32 devices in a mesh: shard: 4 (over z), context: 4 (over y, x), tensor: 2 (over core).
Axes of the slice: x: 2, y: 2, z: 4, core: 2. Of those that a mesh axis runs over, the one named last changes fastest.
Arguments:
- tokens: bfloat16 [4, 1024, 1024], P('shard', 'context'), may hold values from -8 to 8
- segment_ids: int32 [4, 1024], P('shard'), may hold values from 0 to 3, never falling along the last dimension, each value on 1 to 512 neighbouring positions
- norm_gain: bfloat16 [1024], P('shard'), may hold values from 0.5 to 1.5
- in_proj: bfloat16 [1024, 2, 2048], P('shard', None, 'tensor'), may hold values from -0.1875 to 0.1875
- bc_proj: bfloat16 [1024, 256], P('shard'), may hold values from -0.1875 to 0.1875
- dt_proj: bfloat16 [1024, 32], P('shard', 'tensor'), may hold values from -0.1875 to 0.1875
- conv_weight: bfloat16 [4, 32, 64], P(None, 'tensor', 'shard'), may hold values from -3 to 3
- conv_bias: bfloat16 [32, 64], P('tensor', 'shard'), may hold values from -1.75 to 1.75
- bc_conv: bfloat16 [4, 256], P(None, 'shard'), may hold values from -3 to 3
- bc_bias: bfloat16 [256], P('shard'), may hold values from -1.75 to 1.75
- dt_bias: float32 [32], P('tensor'), may hold values from -4 to -1
- a_log: float32 [32], P('tensor'), may hold values from -9 to 0, as said below
- d_skip: float32 [32], P('tensor'), may hold values from 0.5 to 1.5
- out_gain: bfloat16 [32, 64], P('tensor', 'shard'), may hold values from 0.5 to 1.5
- out_proj: bfloat16 [2048, 1024], P('tensor', 'shard'), may hold values from -0.125 to 0.125
- cotangent: bfloat16 [4, 1024, 1024], P('shard', 'context'), may hold values from -8 to 8
Outputs:
- block_out: bfloat16 [4, 1024, 1024], P('shard', 'context', 'tensor')
- tokens_grad: float32 [4, 1024, 1024], P('shard', 'context')
- norm_gain_grad: float32 [1024], P('shard')
- in_proj_grad: float32 [1024, 2, 2048], P('shard', None, 'tensor')
- bc_proj_grad: float32 [1024, 256], P('shard')
- dt_proj_grad: float32 [1024, 32], P('shard', 'tensor')
- conv_weight_grad: float32 [4, 32, 64], P(None, 'tensor', 'shard')
- conv_bias_grad: float32 [32, 64], P('tensor', 'shard')
- bc_conv_grad: float32 [4, 256], P(None, 'shard')
- bc_bias_grad: float32 [256], P('shard')
- dt_bias_grad: float32 [32], P('tensor')
- a_log_grad: float32 [32], P('tensor')
- d_skip_grad: float32 [32], P('tensor')
- out_gain_grad: float32 [32, 64], P('tensor', 'shard')
- out_proj_grad: float32 [2048, 1024], P('tensor', 'shard')
The draws below stay inside these ranges and needn't reach their ends.
Inputs may be any that keep to these rules, and one draw needn't show every extreme that they name: `segment_ids`: numbers never fall along a stream; each stream holds documents 0 to 3, each of 1 to 512 tokens, one exactly 512. `a_log`: one value a head.
All inputs are finite; a program needn't handle non-finite values.
Results may differ from the reference program's by a relative error of at most 0.012.
The reference program's roundings to bfloat16 on the way (of `normed` and `ynorm`) count: a program that leaves them out, or rounds other values in their place, can miss the bound.
Values may be sent and summed in bfloat16 or wider, within the bound.
No kernel may reach another device: no remote copies, remote signals or barrier semaphores. Data moves between devices by JAX's collectives and lax.ppermute only.
A program may use at most 128 MiB of HBM per device.

```python
import math
import jax
import jax.numpy as jnp
import numpy as np
from jax import lax

D = 1024
HEADS = 32
HEADDIM = 64
STATE = 128
CONV = 4
SPAN = 128
DOCS = 4
INNER = 2048
STREAM = 1024
SEQS = 4


def draw_a_log(key, part):
    slowest = math.log(5.0 / STREAM)
    fastest = math.log(max(0.25, 20.0 / STREAM))
    share = jax.random.uniform(key, (HEADS,), jnp.float32)
    lower = slowest
    upper = fastest
    return (lower + share * (upper - lower)).astype(jnp.float32)


def spiked(result, rng, source, target, blocks, factor):
    def block_of(dim):
        return (jnp.arange(result.shape[dim]) // (result.shape[dim] // blocks)).reshape((-1,) + (1,) * (result.ndim - 1 - dim))

    near = jax.random.permutation(rng, blocks)[block_of(target)]
    far = (block_of(target) + blocks // 2) % blocks
    return jnp.where((block_of(source) == near) | (block_of(source) == far), factor * result, result)


def level_of(key, dims, cuts, least, high):
    level = 1.0
    for position, blocks in cuts:
        draws = jax.random.uniform(jax.random.fold_in(jax.random.fold_in(key, 6), position), (blocks,), jnp.float32, least / len(cuts), high / len(cuts))
        level = level * jnp.repeat(jnp.exp(draws), dims[position] // blocks).reshape((-1,) + (1,) * (len(dims) - 1 - position))
    return level


def length_profile(amount, total, limit, slope):
    weights = [(1 << 20) // math.isqrt(standing ** slope) + 1 for standing in range(2, amount + 1)]
    spare, given = total - limit - (amount - 1), [1] * (amount - 1)
    while spare > 0:
        movable = [i for i in range(amount - 1) if given[i] < limit]
        whole, budget = sum([weights[i] for i in movable]), spare
        for i in movable:
            more = min(limit - given[i], max(1, budget * weights[i] // whole), spare)
            given[i] = given[i] + more
            spare = spare - more
    return np.array([limit] + given)


def uneven_parts(own_key, count, total, most, skew):
    if count == 2:
        one = jax.random.randint(own_key, (), max(1, total - most), min(most, total - 1) + 1)
        return jnp.stack([one, total - one])
    lengths = jnp.asarray(length_profile(count, total, most, skew), jnp.int32)
    pairs = (count - 1) // 2
    donor, receiver = lengths[1:1 + 2 * pairs:2], lengths[2:2 + 2 * pairs:2]
    margin = jnp.minimum(donor - 1, most - receiver)
    moved = jax.random.randint(jax.random.fold_in(own_key, 1), (pairs,), 0, 1 << 20) % (margin + 1)
    lengths = lengths.at[1:1 + 2 * pairs:2].set(donor - moved).at[2:2 + 2 * pairs:2].set(receiver + moved)
    return lengths[jax.random.permutation(jax.random.fold_in(own_key, 2), count)]


def scatter_about(rng, dims, scale, bound, pieces=(), kind=jnp.bfloat16):
    values = scale * jax.random.normal(rng, dims, jnp.float32)
    if pieces:
        values = values * level_of(rng, dims, pieces, -0.22, 0.18)
    return jnp.clip(values, -bound, bound).astype(kind)


def noise_with(own_key, shape, deviation, limit, split, heavy, kind=jnp.bfloat16):
    values = deviation * jax.random.normal(own_key, shape, jnp.float32)
    if split:
        values = values * level_of(own_key, shape, split, -0.22, 0.18)
    return jnp.clip(spiked(values, jax.random.fold_in(own_key, 3), *heavy), -limit, limit).astype(kind)


def setup_inputs(seed: int = 0) -> dict:
    splits = jax.random.split(jax.random.key(seed), 17)
    return {
        "tokens": noise_with(splits[0], (SEQS, STREAM, D), 1.0, 8.0, ((0, 4), (1, 4)), (0, 2, 4, 2.0)),
        "segment_ids": jax.vmap(lambda own: jnp.searchsorted(jnp.cumsum(uneven_parts(own, DOCS, STREAM, STREAM // 2, 0)), jnp.arange(STREAM), side="right"))(jax.random.split(splits[1], SEQS)).reshape((SEQS, STREAM)).astype(jnp.int32),
        "norm_gain": jnp.clip(1.0 + 0.1 * jax.random.normal(splits[2], (D,), jnp.float32), 0.5, 1.5).astype(jnp.bfloat16),
        "in_proj": scatter_about(splits[3], (D, 2, INNER), D ** -0.5, 0.1875, ((0, 4), (2, 2))),
        "bc_proj": scatter_about(splits[4], (D, 2 * STATE), D ** -0.5, 0.1875, ((0, 4),)),
        "dt_proj": scatter_about(splits[5], (D, HEADS), D ** -0.5, 0.1875, ((0, 4), (1, 2))),
        "conv_weight": scatter_about(splits[6], (CONV, HEADS, HEADDIM), CONV ** -0.5, 3.0, ((1, 2), (2, 4))),
        "conv_bias": scatter_about(splits[7], (HEADS, HEADDIM), 0.3, 1.75, ((0, 2), (1, 4))),
        "bc_conv": scatter_about(splits[8], (CONV, 2 * STATE), CONV ** -0.5, 3.0, ((1, 4),)),
        "bc_bias": scatter_about(splits[9], (2 * STATE,), 0.3, 1.75, ((0, 4),)),
        "dt_bias": jnp.clip(-4.0 + 3.0 * jax.random.uniform(splits[10], (HEADS,), jnp.float32) ** level_of(splits[10], (HEADS,), ((0, 2),), -0.2, 0.2), -4.0, -1.0),
        "a_log": draw_a_log(jax.random.fold_in(splits[16], 71), 0),
        "d_skip": jnp.clip(0.5 + 1.0 * jax.random.uniform(splits[12], (HEADS,), jnp.float32) ** level_of(splits[12], (HEADS,), ((0, 2),), -0.2, 0.2), 0.5, 1.5),
        "out_gain": jnp.clip(1.0 + 0.1 * jax.random.normal(splits[13], (HEADS, HEADDIM), jnp.float32), 0.5, 1.5).astype(jnp.bfloat16),
        "out_proj": scatter_about(splits[14], (INNER, D), INNER ** -0.5, 0.125, ((0, 2), (1, 4))),
        "cotangent": noise_with(splits[15], (SEQS, STREAM, D), 1.0, 8.0, ((0, 4), (1, 4)), (0, 2, 4, 2.0)),
    }


eps = 1e-05
highest = lax.Precision.HIGHEST

def front(values, gain):
    return values * lax.rsqrt(lax.optimization_barrier(jnp.mean(values * values, -1, keepdims=True)) + eps) * gain

def causal_conv(extended, kernel, offset, segwin, length):
    total = jnp.zeros_like(extended[CONV - 1:]) + offset
    for tap in range(CONV):
        same = (segwin[tap:tap + length] == segwin[CONV - 1:]).astype(extended.dtype)
        total = total + kernel[tap] * extended[tap:tap + length] * same[:, None]
    return total

def span_scan(xval, bmat, cmat, dtval, decay, reset, start):
    length, heads, head_dim = xval.shape
    count = length // SPAN

    def blocks(array):
        return array.reshape((count, SPAN) + array.shape[1:])
    order = jnp.arange(SPAN)
    causal = order[:, None] >= order[None, :]

    def advance(state, block):
        xblock, bblock, cblock, dblock, ablock, rblock = block
        acum = jnp.cumsum(ablock, axis=0)
        rcum = jnp.cumsum(rblock)
        keep = causal & (rcum[:, None] == rcum[None, :])
        diff = acum.T[:, :, None] - acum.T[:, None, :]
        weight = jnp.exp(jnp.where(keep[None], diff, -jnp.inf))
        scores = jnp.dot(cblock, bblock.T, precision=highest)
        mixing = weight * scores[None] * dblock.T[:, None, :]
        inner = jnp.einsum('hts,shp->thp', mixing, xblock, precision=highest)
        carry = jnp.exp(acum) * (rcum == 0.0).astype(acum.dtype)[:, None]
        outer = carry[:, :, None] * jnp.einsum('tn,hpn->thp', cblock, state, precision=highest)
        tail = jnp.exp(acum[-1][None, :] - acum) * (rcum == rcum[-1]).astype(acum.dtype)[:, None] * dblock
        fresh = jnp.einsum('sh,shp,sn->hpn', tail, xblock, bblock, precision=highest)
        return (carry[-1][:, None, None] * state + fresh, inner + outer)
    final, outputs = lax.scan(advance, start, (blocks(xval), blocks(bmat), blocks(cmat), blocks(dtval), blocks(decay), blocks(reset)))
    return (final, outputs.reshape(length, heads, head_dim))

def mixer(zvalue, xpre, bcpre, dtraw, kernel_x, offset_x, kernel_bc, offset_bc, step_bias, log_rate, skip_gain, gate_gain, segments):
    length = zvalue.shape[0]
    padseg = jnp.concatenate([jnp.full((CONV - 1,), -1, jnp.int32), segments.astype(jnp.int32)])
    ext_x = jnp.concatenate([jnp.zeros((CONV - 1, xpre.shape[1]), jnp.float32), xpre], 0)
    ext_bc = jnp.concatenate([jnp.zeros((CONV - 1, bcpre.shape[1]), jnp.float32), bcpre], 0)
    xact = jax.nn.silu(causal_conv(ext_x, kernel_x, offset_x, padseg, length))
    bcact = jax.nn.silu(causal_conv(ext_bc, kernel_bc, offset_bc, padseg, length))
    dtval = jax.nn.softplus(dtraw + step_bias)
    decay = -jnp.exp(log_rate) * dtval
    reset = (padseg[CONV - 1:] != padseg[CONV - 2:-1]).astype(jnp.float32)
    xval = xact.reshape(length, HEADS, HEADDIM)
    start = jnp.zeros((HEADS, HEADDIM, STATE), jnp.float32)
    final, ssd = span_scan(xval, bcact[:, :STATE], bcact[:, STATE:], dtval, decay, reset, start)
    ssd = ssd + skip_gain[None, :, None] * xval
    gated = ssd.reshape(length, INNER) * jax.nn.silu(zvalue)
    scale = lax.rsqrt(lax.optimization_barrier(jnp.mean(gated * gated, -1, keepdims=True)) + eps)
    return gated * scale * gate_gain

def reference(tokens, segment_ids, norm_gain, in_proj, bc_proj, dt_proj, conv_weight, conv_bias, bc_conv, bc_bias, dt_bias, a_log, d_skip, out_gain, out_proj, cotangent):
    inner_weight = in_proj.reshape(D, 2 * INNER)
    gain = norm_gain.astype(jnp.float32)
    params = (conv_weight.reshape(CONV, INNER).astype(jnp.float32), conv_bias.reshape(INNER).astype(jnp.float32), bc_conv.astype(jnp.float32), bc_bias.astype(jnp.float32), dt_bias, a_log, d_skip, out_gain.reshape(INNER).astype(jnp.float32))

    def stream(totals, item):
        xrow, segrow, cotrow = item
        xfloat = xrow.astype(jnp.float32)
        normed = front(xfloat, gain).astype(jnp.bfloat16)
        zxvalue = jnp.dot(normed, inner_weight, preferred_element_type=jnp.float32)
        zvalue = zxvalue[:, :INNER]
        xpre = zxvalue[:, INNER:].astype(jnp.bfloat16)
        bcpre = jnp.dot(normed, bc_proj, preferred_element_type=jnp.float32).astype(jnp.bfloat16)
        dtraw = jnp.dot(normed, dt_proj, preferred_element_type=jnp.float32)

        def local(*values):
            return mixer(*values, segrow)
        yfull, pullback = jax.vjp(local, zvalue, xpre.astype(jnp.float32), bcpre.astype(jnp.float32), dtraw, *params)
        ynorm = yfull.astype(jnp.bfloat16)
        output = jnp.dot(ynorm, out_proj, preferred_element_type=jnp.float32)
        block = (xfloat + output).astype(jnp.bfloat16)
        dynorm = jnp.dot(cotrow, out_proj.T, preferred_element_type=jnp.float32)
        grads = pullback(dynorm)
        dzx = jnp.concatenate([grads[0], grads[1]], 1).astype(jnp.bfloat16)
        dbc = grads[2].astype(jnp.bfloat16)
        ddt = grads[3].astype(jnp.bfloat16)
        dnormed = jnp.dot(dzx, inner_weight.T, preferred_element_type=jnp.float32) + jnp.dot(dbc, bc_proj.T, preferred_element_type=jnp.float32) + jnp.dot(ddt, dt_proj.T, preferred_element_type=jnp.float32)
        unused, back = jax.vjp(front, xfloat, gain)
        dxfloat, dgain = back(dnormed)
        terms = (dgain, jnp.dot(normed.T, dzx, preferred_element_type=jnp.float32), jnp.dot(normed.T, dbc, preferred_element_type=jnp.float32), jnp.dot(normed.T, ddt, preferred_element_type=jnp.float32)) + tuple(grads[4:]) + (jnp.dot(ynorm.T, cotrow, preferred_element_type=jnp.float32),)
        totals = tuple((left + right for left, right in zip(totals, terms)))
        return (totals, (block, cotrow.astype(jnp.float32) + dxfloat))
    shapes = [(D,), (D, 2 * INNER), (D, 2 * STATE), (D, HEADS), (CONV, INNER), (INNER,), (CONV, 2 * STATE), (2 * STATE,), (HEADS,), (HEADS,), (HEADS,), (INNER,), (INNER, D)]
    initial = tuple((jnp.zeros(shape, jnp.float32) for shape in shapes))
    totals, outputs = lax.scan(stream, initial, (tokens, segment_ids, cotangent))
    block_out, tokens_grad = outputs
    return (block_out, tokens_grad, totals[0], totals[1].reshape(D, 2, INNER), totals[2], totals[3], totals[4].reshape(CONV, HEADS, HEADDIM), totals[5].reshape(HEADS, HEADDIM), totals[6], totals[7], totals[8], totals[9], totals[10], totals[11].reshape(HEADS, HEADDIM), totals[12])
```

```python
import jax
import jax.numpy as jnp
from jax import lax
from jax.experimental import pallas as pl
from jax.experimental.pallas import tpu as pltpu
from jax.sharding import PartitionSpec as P

CONV = 4
SPAN = 128
PAD = 16
GAIN = 8
HEADP = 16
BCP = 24
RATE = 32
MISC = 128
eps = 1e-05
f32 = jnp.float32
bf16 = jnp.bfloat16


def mm(a, b, ca=1, cb=0):
    return lax.dot_general(a, b, (((ca,), (cb,)), ((), ())), preferred_element_type=f32)


def pieces(x, count):
    parts = []
    for _ in range(count):
        part = x.astype(bf16)
        parts.append(part)
        x = x - part.astype(f32)
    return parts


def exact_left(ones, x, count, cb=0):
    return sum(mm(ones, part, 1, cb) for part in pieces(x, count))


def exact_right(x, ones, count, ca=1, cb=0):
    return sum(mm(part, ones, ca, cb) for part in pieces(x, count))


def iota(shape, dim):
    return lax.broadcasted_iota(jnp.int32, shape, dim)


def low(x, size):
    return lax.bitwise_and(x, jnp.int32(size - 1))


def high(x, size):
    return lax.shift_right_logical(x, jnp.int32(size.bit_length() - 1))


def sigmoid(x):
    return 1.0 / (1.0 + jnp.exp(-x))


def softplus(x):
    return jnp.maximum(x, 0.0) + jnp.log1p(jnp.exp(-jnp.abs(x)))


def spread_head(width, shards, channels, head):
    rows = width // shards
    part = head // shards
    used = (channels // head) * part
    r, c = iota((width, channels), 0), iota((width, channels), 1)
    s, q = high(r, rows), low(r, rows)
    hit = (c == high(q, part) * head + s * part + low(q, part)) & (q < used)
    return hit.astype(f32).astype(bf16)


def spread_bc(width, shards, channels):
    rows = width // shards
    part = channels // shards
    r, c = iota((width, channels), 0), iota((width, channels), 1)
    s, q = high(r, rows), low(r, rows)
    return ((c == s * part + q) & (q < part)).astype(f32).astype(bf16)


def spread_rate(width, shards, channels, head):
    rows = width // shards
    r, c = iota((width, channels), 0), iota((width, channels), 1)
    q = low(r, rows)
    return ((c == q * head) & (q < channels // head)).astype(f32).astype(bf16)


def block_ones(channels, head):
    r, c = iota((channels, channels), 0), iota((channels, channels), 1)
    return (high(r, head) == high(c, head)).astype(f32).astype(bf16)


def one_hot(rows, cols, row, col):
    return ((iota((rows, cols), 0) == row) & (iota((rows, cols), 1) == col)).astype(f32).astype(bf16)


def triangle(lower):
    r, c = iota((SPAN, SPAN), 0), iota((SPAN, SPAN), 1)
    hit = (r >= c) if lower else (r <= c)
    return hit.astype(f32).astype(bf16)


def local_decay(keep, a, at, head, h):
    diff = a[:, h * head : h * head + 1] - at[h * head : h * head + 1, :]
    return jnp.exp(jnp.where(keep, diff, -1e30))


def front_kernel(dims, *refs):
    shards, contexts, head, channels, state = dims
    it = iter(refs)
    idx = next(it)
    segr, masks, rates = next(it), next(it), next(it)
    own = next(it)
    mine = [next(it) for _ in range(contexts - 1)]
    other = [next(it) for _ in range(contexts - 1)]
    wparts = [next(it) for _ in range(shards)]
    bcother = next(it)
    normed, wfull, small, pre, uall, dtraw, ssd, states = (next(it) for _ in range(8))
    wdt, sref, pref = (next(it) for _ in range(3))
    c, t, s = idx[0], idx[1], idx[2]
    length, width = own.shape
    half = length // 2
    total = length * contexts
    rows = width // shards
    bcw = 2 * state
    for k in range(shards):
        at = pl.multiple_of((s ^ k) * rows, rows)
        part = wparts[k]
        wfull[pl.ds(at, rows), 0:channels] = part[:, 0:channels]
        here, there = part[:, channels : channels + state], bcother[k]
        wfull[pl.ds(at, rows), channels : channels + state] = jnp.where(t == 0, here, there)
        wfull[pl.ds(at, rows), channels + state : channels + bcw] = jnp.where(t == 0, there, here)
        wfull[pl.ds(at, rows), channels + bcw :] = part[:, channels + state :]
    misc = wfull[:, channels + bcw :]
    small[0:MISC, :] = mm(misc, spread_head(width, shards, channels, head), 0, 0)
    small[MISC:, :] = mm(misc, spread_bc(width, shards, bcw), 0, 0)
    expand = (iota((MISC, channels), 0) == high(iota((MISC, channels), 1), head)).astype(f32)
    wdt[...] = mm(misc, expand.astype(bf16)).astype(bf16)
    gain = mm(one_hot(8, MISC, 0, GAIN), misc, 1, 1)[0:1, :]

    def norm(tokens):
        x = tokens.astype(f32)
        return (x * lax.rsqrt(jnp.mean(x * x, -1, keepdims=True) + eps) * gain).astype(bf16)

    for q in range(length // SPAN):
        normed[pl.ds(pl.multiple_of(c * length + q * SPAN, SPAN), SPAN), :] = norm(
            own[q * SPAN : (q + 1) * SPAN, :]
        )
    for k in range(1, contexts):
        base = (c ^ k) * length
        normed[pl.ds(pl.multiple_of(base + t * half, half), half), :] = norm(mine[k - 1][...])
        normed[pl.ds(pl.multiple_of(base + (1 - t) * half, half), half), :] = norm(other[k - 1][...])
    pref[0:PAD, :] = jnp.zeros((PAD, channels + bcw), f32)
    pre[0:PAD, :] = jnp.zeros((PAD, channels + bcw), bf16)
    chunk = 2 * SPAN

    def project(i, _):
        at = pl.multiple_of(i * chunk, chunk)
        n = normed[pl.ds(at, chunk), :]
        value = mm(n, wfull[:, 0 : channels + bcw]).astype(bf16)
        pre[pl.ds(pl.multiple_of(at + PAD, PAD), chunk), :] = value
        pref[pl.ds(pl.multiple_of(at + PAD, PAD), chunk), :] = value.astype(f32)
        dtraw[pl.ds(at, chunk), :] = mm(n, wdt[...])
        return 0

    lax.fori_loop(0, total // chunk, project, 0)
    sref[...] = jnp.zeros_like(sref)
    tri = triangle(True)
    causal = iota((SPAN, SPAN), 0) >= iota((SPAN, SPAN), 1)
    side = iota((SPAN, 2 * head), 1) < head

    def scan(i, _):
        at = pl.multiple_of(i * SPAN, SPAN)
        window = pref[pl.ds(at, SPAN + PAD), :]
        mk = masks[pl.ds(at, SPAN), :]
        taps = jnp.concatenate(
            [small[HEADP : HEADP + 8, :], small[MISC + BCP : MISC + BCP + 8, :]], 1
        )
        u = taps[CONV - 1 : CONV, :] * window[PAD:, :]
        bias = jnp.concatenate(
            [small[HEADP + 4 : HEADP + 5, :], small[MISC + BCP + 4 : MISC + BCP + 5, :]], 1
        )
        u = u + bias
        for j in range(1, CONV):
            u = u + taps[CONV - 1 - j : CONV - j, :] * (
                window[PAD - j : PAD - j + SPAN, :] * mk[:, j - 1 : j]
            )
        uall[pl.ds(at, SPAN), :] = u
        act = u * sigmoid(u)
        x = act[:, 0:channels]
        bb = act[:, channels : channels + state].astype(bf16)
        cb = act[:, channels + state :].astype(bf16)
        dt = softplus(dtraw[pl.ds(at, SPAN), :] + rates[0:1, :])
        a = exact_left(tri, rates[1:2, :] * dt, 3)
        att = a.T
        step = x * dt
        ub = step.astype(bf16)
        g = mm(cb, bb, 1, 1)
        keep = (mk[:, 5:6] == segr[pl.ds(i, 1), :]) & causal
        inner = []
        for pair in range(channels // (2 * head)):
            up = ub[:, pair * 2 * head : (pair + 1) * 2 * head]
            both = [
                mm((g * local_decay(keep, a, att, head, 2 * pair + e)).astype(bf16), up)
                for e in range(2)
            ]
            inner.append(jnp.where(side, both[0], both[1]))
        before = sref[...]
        sb = before.astype(bf16)
        states[pl.ds(pl.multiple_of(i * channels, channels), channels), :] = sb
        carry = jnp.exp(a) * mk[:, 3:4]
        y = jnp.concatenate(inner, 1) + carry * mm(cb, sb, 1, 1)
        ssd[pl.ds(at, SPAN), :] = y + rates[2:3, :] * x
        tail = jnp.exp(a[SPAN - 1 :, :] - a) * mk[:, 4:5]
        through = jnp.exp(att[:, SPAN - 1 :]) * mk[SPAN - 1 :, 3:4]
        sref[...] = through * before + mm((tail * step).astype(bf16), bb, 0, 0)
        return 0

    lax.fori_loop(0, total // SPAN, scan, 0)


def assemble_tokens(dst, idx, own, mine, other):
    c, t = idx[0], idx[1]
    length = own.shape[0]
    half = length // 2
    dst[pl.ds(pl.multiple_of(c * length, length), length), :] = own[...]
    for k in range(1, len(mine) + 1):
        base = (c ^ k) * length
        dst[pl.ds(pl.multiple_of(base + t * half, half), half), :] = mine[k - 1][...]
        dst[pl.ds(pl.multiple_of(base + (1 - t) * half, half), half), :] = other[k - 1][...]


def gate_kernel(dims, *refs):
    shards, contexts, head, channels, state = dims
    it = iter(refs)
    idx = next(it)
    normed, ssd, small = next(it), next(it), next(it)
    own = next(it)
    mine = [next(it) for _ in range(contexts - 1)]
    other = [next(it) for _ in range(contexts - 1)]
    wparts = [next(it) for _ in range(shards)]
    sums, cot, wzo, zval, dyn = (next(it) for _ in range(5))
    s = idx[2]
    width = normed.shape[1]
    rows = width // shards
    for k in range(shards):
        wzo[pl.ds(pl.multiple_of((s ^ k) * rows, rows), rows), :] = wparts[k][...]
    assemble_tokens(cot, idx, own, mine, other)
    chunk = 2 * SPAN
    ogain = small[HEADP + 5 : HEADP + 6, :]
    ones = jnp.ones((8, channels), bf16)
    for i in range(normed.shape[0] // chunk):
        at = slice(i * chunk, (i + 1) * chunk)
        z = mm(normed[at, :], wzo[:, 0:channels])
        d = mm(cot[at, :], wzo[:, channels:])
        zval[at, :] = z
        dyn[at, :] = d
        gated = ssd[at, :] * (z * sigmoid(z))
        sums[0:1, at] = exact_left(ones, gated * gated, 2, 1)[0:1, :]
        sums[1:2, at] = exact_left(ones, d * ogain * gated, 2, 1)[0:1, :]


def mid_kernel(dims, inner, *refs):
    shards, contexts, head, channels, state = dims
    it = iter(refs)
    idx = next(it)
    sums, normed, ssd, small, cot, wzo, zval, dyn = (next(it) for _ in range(8))
    okeep, osend, dz, dssd, ogg = (next(it) for _ in range(5))
    gparts = [next(it) for _ in range(shards)]
    yref = next(it)
    t, s = idx[1], idx[2]
    total, width = normed.shape
    rows = width // shards
    part = width // 2
    chunk = 2 * SPAN
    ogain = small[HEADP + 5 : HEADP + 6, :]
    first = (iota((8, channels), 0) == 0).astype(f32).astype(bf16)
    second = (iota((8, channels), 0) == 1).astype(f32).astype(bf16)
    gacc = jnp.zeros((1, channels), f32)
    keep_at = pl.multiple_of(t * part, part)
    send_at = pl.multiple_of((1 - t) * part, part)
    for i in range(total // chunk):
        at = slice(i * chunk, (i + 1) * chunk)
        pair = jnp.concatenate([sums[:, at], jnp.zeros((6, chunk), f32)], 0)
        square = exact_right(pair, first, 3, 0, 0)
        cross = exact_right(pair, second, 3, 0, 0)
        z = zval[at, :]
        sg = sigmoid(z)
        zs = z * sg
        out = ssd[at, :]
        gated = out * zs
        r = lax.rsqrt(square / inner + eps)
        ynorm = (gated * r * ogain).astype(bf16)
        yref[at, :] = ynorm
        okeep[at, :] = mm(ynorm, wzo[pl.ds(keep_at, part), channels:], 1, 1).astype(bf16)
        osend[at, :] = mm(ynorm, wzo[pl.ds(send_at, part), channels:], 1, 1).astype(bf16)
        d = dyn[at, :]
        dgated = r * (d * ogain) - gated * (r * r * r) * (cross / inner)
        dssd[at, :] = dgated * zs
        dz[at, :] = (dgated * out * (sg * (1.0 + z * (1.0 - sg)))).astype(bf16)
        gacc = gacc + jnp.sum(d * gated * r, 0, keepdims=True)
    ogg[...] = jnp.broadcast_to(gacc, ogg.shape)
    for k in range(shards):
        at = pl.multiple_of((s ^ k) * rows, MISC)
        gparts[k][:, 0:channels] = mm(normed[:, pl.ds(at, rows)], dz[...], 0, 0).astype(bf16)
        gparts[k][:, channels:] = mm(cot[:, pl.ds(at, rows)], yref[...], 0, 0).astype(bf16)


def back_kernel(dims, *refs):
    shards, contexts, head, channels, state = dims
    it = iter(refs)
    idx = next(it)
    segr, masks, rates = next(it), next(it), next(it)
    normed, wfull, small, pre, uall, dtraw, ssd, states = (next(it) for _ in range(8))
    wzo, dz, dssd, ogg = (next(it) for _ in range(4))
    dkeep, dsend, gkeep, gsend = (next(it) for _ in range(4))
    dcat, dsref, acc = (next(it) for _ in range(3))
    t = idx[1]
    total, width = normed.shape
    bcw = 2 * state
    cat = channels + bcw
    blocks = total // SPAN
    dsref[...] = jnp.zeros_like(dsref)
    acc[...] = jnp.zeros_like(acc)
    lower, upper = triangle(True), triangle(False)
    ones = block_ones(channels, head)
    causal = iota((SPAN, SPAN), 0) >= iota((SPAN, SPAN), 1)
    side = iota((SPAN, 2 * head), 1) < head
    last = iota((SPAN, channels), 0) == SPAN - 1
    sel = (
        iota((channels, MISC), 0) == iota((channels, MISC), 1) * head
    ).astype(f32).astype(bf16)
    row8 = jnp.ones((8, state), bf16)

    def step(ii, halo):
        i = blocks - 1 - ii
        at = pl.multiple_of(i * SPAN, SPAN)
        here = pl.ds(at, SPAN)
        mk = masks[pl.ds(at, SPAN + PAD), :]
        mh = mk[0:SPAN, :]
        u = uall[here, :]
        sg = sigmoid(u)
        act = u * sg
        x = act[:, 0:channels]
        bb = act[:, channels : channels + state].astype(bf16)
        cb = act[:, channels + state :].astype(bf16)
        raw = dtraw[here, :] + rates[0:1, :]
        dt = softplus(raw)
        dec = rates[1:2, :] * dt
        a = exact_left(lower, dec, 3)
        att = a.T
        us = x * dt
        ub = us.astype(bf16)
        dy = dssd[here, :]
        dyb = dy.astype(bf16)
        g = mm(cb, bb, 1, 1)
        keep = (mh[:, 5:6] == segr[pl.ds(i, 1), :]) & causal
        carry = jnp.exp(a) * mh[:, 3:4]
        tail = jnp.exp(a[SPAN - 1 :, :] - a) * mh[:, 4:5]
        sb = states[pl.ds(pl.multiple_of(i * channels, channels), channels), :]
        nxt = jnp.minimum(i + 1, blocks - 1)
        snext = states[pl.ds(pl.multiple_of(nxt * channels, channels), channels), :].astype(f32)
        dsn = dsref[...]
        dsb = dsn.astype(bf16)
        cdy = (carry * dy).astype(bf16)
        tu = (tail * us).astype(bf16)
        dg = jnp.zeros((SPAN, SPAN), f32)
        dus = []
        for pair in range(channels // (2 * head)):
            lanes = slice(pair * 2 * head, (pair + 1) * 2 * head)
            up, dyp = ub[:, lanes], dyb[:, lanes]
            both = []
            for e in range(2):
                decay = local_decay(keep, a, att, head, 2 * pair + e)
                mine = side if e == 0 else jnp.logical_not(side)
                dm = mm(dyp, jnp.where(mine, up, jnp.zeros_like(up)), 1, 1)
                dg = dg + dm * decay
                both.append(mm((g * decay).astype(bf16), dyp, 0, 0))
            dus.append(jnp.where(side, both[0], both[1]))
        dgb = dg.astype(bf16)
        dc = mm(dgb, bb) + mm(cdy, sb)
        db = mm(dgb, cb, 0, 0) + mm(tu, dsb)
        du = jnp.concatenate(dus, 1) + tail * mm(bb, dsb, 1, 1)
        through = jnp.exp(att[:, SPAN - 1 :]) * mh[SPAN - 1 :, 3:4]
        dsref[...] = through * dsn + mm(cdy, cb, 0, 0)
        y = ssd[here, :] - rates[2:3, :] * x
        extra = exact_left(row8, snext * dsn, 3, 1)[0:1, :]
        e = dyb.astype(f32) * y - ub.astype(f32) * du
        e = e + jnp.where(last, extra, 0.0)
        ddec = exact_right(exact_left(upper, e, 3), ones, 3)
        xdu = exact_right(x * du, ones, 2)
        ddt = (xdu + rates[1:2, :] * ddec) * sigmoid(raw)
        acc[8:9, :] = acc[8:9, :] + jnp.sum(ddt, 0, keepdims=True)
        acc[9:10, :] = acc[9:10, :] + jnp.sum(ddec * dec, 0, keepdims=True)
        acc[10:11, :] = acc[10:11, :] + jnp.sum(dy * x, 0, keepdims=True)
        dx = dt * du + rates[2:3, :] * dy
        dact = jnp.concatenate([dx, db, dc], 1)
        dut = dact * (sg * (1.0 + u * (1.0 - sg)))
        dwin = jnp.concatenate([dut, halo], 0)
        pwin = pre[pl.ds(at, SPAN + PAD), :].astype(f32)
        taps = jnp.concatenate(
            [small[HEADP : HEADP + 8, :], small[MISC + BCP : MISC + BCP + 8, :]], 1
        )
        dpre = taps[CONV - 1 : CONV, :] * dut

        def gather(row, value):
            total_row = jnp.sum(value, 0, keepdims=True)
            acc[row : row + 1, :] = acc[row : row + 1, :] + total_row[:, 0:channels]
            acc[16 + row : 17 + row, 0:bcw] = acc[16 + row : 17 + row, 0:bcw] + total_row[:, channels:]

        gather(CONV - 1, dut * pwin[PAD:, :])
        gather(CONV, dut)
        for j in range(1, CONV):
            moved = dwin * mk[:, j - 1 : j]
            dpre = dpre + taps[CONV - 1 - j : CONV - j, :] * moved[j : j + SPAN, :]
            gather(CONV - 1 - j, moved[0:SPAN, :] * pwin[PAD - j : PAD - j + SPAN, :])
        dcat[here, 0:cat] = dpre.astype(bf16)
        dcat[here, cat:] = mm(ddt.astype(bf16), sel).astype(bf16)
        return dut[0:PAD, :]

    lax.fori_loop(0, blocks, step, jnp.zeros((PAD, cat), f32))
    part = width // 2
    keep_at = pl.multiple_of(t * part, part)
    send_at = pl.multiple_of((1 - t) * part, part)
    gain8 = mm(one_hot(8, MISC, 0, GAIN), wfull[:, cat:], 1, 1)[0:1, :]
    chunk = 2 * SPAN
    ng = jnp.zeros((1, width), f32)
    for i in range(total // chunk):
        at = slice(i * chunk, (i + 1) * chunk)
        full = mm(dcat[at, :], wfull[...], 1, 1) + mm(dz[at, :], wzo[:, 0:channels], 1, 1)
        ng = ng + jnp.sum(full * normed[at, :].astype(f32), 0, keepdims=True)
        lo, hi = full[:, 0:part].astype(bf16), full[:, part:].astype(bf16)
        dkeep[at, :] = jnp.where(t == 0, lo, hi)
        dsend[at, :] = jnp.where(t == 0, hi, lo)
    ng = ng / gain8
    sums = acc[8:16, :]
    rate = exact_right(sums, ones, 3)
    line = iota((8, channels), 0)
    rate = jnp.where(line == 2, rate, sums)
    headg = jnp.where(line == 5, ogg[0:8, :], acc[0:8, :])
    z8 = jnp.zeros((8, channels), f32)

    def place(rowsets, spread):
        stack = [z8] * (MISC // 8)
        for row, value in rowsets:
            stack[row // 8] = value
        return mm(spread, jnp.concatenate(stack, 0).astype(bf16), 1, 1)

    misc = place([(HEADP, headg)], spread_head(width, shards, channels, head))
    misc = misc + place([(BCP, acc[16:24, 0:bcw])], spread_bc(width, shards, bcw))
    misc = misc + place([(RATE, rate)], spread_rate(width, shards, channels, head))
    ng8 = jnp.concatenate([ng, jnp.zeros((7, width), f32)], 0)
    misc = misc + exact_right(ng8, one_hot(8, MISC, 0, GAIN), 2, 0, 0)
    for i in range(width // chunk):
        at = slice(i * chunk, (i + 1) * chunk)
        gw = mm(normed[:, at], dcat[...], 0, 0)
        gkeep[at, 0:channels] = gw[:, 0:channels].astype(bf16)
        b, c = gw[:, channels : channels + state], gw[:, channels + state : cat]
        gkeep[at, channels : channels + state] = jnp.where(t == 0, b, c).astype(bf16)
        gsend[at, 0:state] = jnp.where(t == 0, c, b).astype(bf16)
        m = (gw[:, cat:] + misc[at, :]).astype(bf16)
        gkeep[at, channels + state :] = m
        gsend[at, state:] = m


def swap(x, axis, k):
    return lax.ppermute(x, axis, [(i, i ^ k) for i in range(lax.axis_size(axis))])


def call(body, args, outs, scratch):
    smem = pl.BlockSpec(memory_space=pltpu.SMEM)
    vmem = pl.BlockSpec(memory_space=pltpu.VMEM)
    return pl.pallas_call(
        body,
        out_shape=[jax.ShapeDtypeStruct(s, d) for s, d in outs],
        in_specs=[smem] + [vmem] * (len(args) - 1),
        out_specs=[vmem] * len(outs),
        scratch_shapes=[pltpu.VMEM(s, d) for s, d in scratch],
        compiler_params=pltpu.CompilerParams(vmem_limit_bytes=56 << 20),
    )(*args)


def ordered(parts, place):
    stack = jnp.stack(parts)
    return [lax.dynamic_index_in_dim(stack, place ^ j, 0, False) for j in range(len(parts))]


def stream_parts(rows, core, contexts):
    half = rows.shape[0] // 2
    mine = lax.dynamic_slice_in_dim(rows, core * half, half, 0)
    return [swap(mine, "context", k) for k in range(1, contexts)]


def on_device(
    tokens,
    segment_ids,
    norm_gain,
    in_proj,
    bc_proj,
    dt_proj,
    conv_weight,
    conv_bias,
    bc_conv,
    bc_bias,
    dt_bias,
    a_log,
    d_skip,
    out_gain,
    out_proj,
    cotangent,
):
    shards, contexts = lax.axis_size("shard"), lax.axis_size("context")
    s, c, t = lax.axis_index("shard"), lax.axis_index("context"), lax.axis_index("tensor")
    idx = jnp.stack([c, t, s]).astype(jnp.int32)
    length, width = tokens.shape[1:]
    total = length * contexts
    rows = in_proj.shape[0]
    heads = dt_bias.shape[0] // contexts
    state = bc_proj.shape[1] // 2
    bcw = 2 * state
    channels = in_proj.shape[2] // contexts
    head = channels // heads
    inner = in_proj.shape[2] * lax.axis_size("tensor")
    dims = (shards, contexts, head, channels, state)
    own, cot = tokens[0], cotangent[0]

    def mine(x, dim, size):
        return lax.dynamic_slice_in_dim(x, c * size, size, dim)

    tok_mine = stream_parts(own, t, contexts)
    both = lax.dynamic_slice(in_proj, (0, 0, c * channels), (rows, 2, channels))
    hparts = [
        mine(conv_weight, 1, heads).reshape(CONV, -1),
        mine(conv_bias, 0, heads).reshape(1, -1),
        mine(out_gain, 0, heads).reshape(1, -1),
    ]
    headp = jnp.concatenate(hparts, 0).T
    bcp = jnp.concatenate([bc_conv, bc_bias[None]], 0).T

    def column(x, at):
        return jnp.pad(x, ((0, rows - x.shape[0]), (at, MISC - at - x.shape[1])))

    misc = (
        column(mine(dt_proj, 1, heads), 0)
        + column(norm_gain[:, None], GAIN)
        + column(headp, HEADP)
        + column(bcp, BCP)
    )
    wa = jnp.concatenate(
        [both[:, 1], lax.dynamic_slice_in_dim(bc_proj, t * state, state, 1), misc], 1
    )
    wa_parts = [wa] + [swap(wa, "shard", k) for k in range(1, shards)]
    bc_other = swap(
        jnp.stack([w[:, channels : channels + state] for w in wa_parts]), "tensor", 1
    )
    tok_other = [swap(x, "tensor", 1) for x in tok_mine]
    cot_mine = stream_parts(cot, t, contexts)
    wo = mine(out_proj, 0, channels).T
    wb = jnp.concatenate([both[:, 0], wo], 1)
    wb_parts = [wb] + [swap(wb, "shard", k) for k in range(1, shards)]
    cot_other = [swap(x, "tensor", 1) for x in cot_mine]

    seg = segment_ids[0]
    cols = []
    for j in range(1, CONV):
        moved = jnp.concatenate([jnp.full((j,), -1, jnp.int32), seg[:-j]])
        cols.append((moved == seg).astype(f32))
    grid = seg.reshape(total // SPAN, SPAN)
    previous = jnp.concatenate([jnp.full((1,), -1, jnp.int32), grid[:-1, -1]])
    cols.append((grid == previous[:, None]).astype(f32).reshape(-1))
    cols.append((grid == grid[:, -1:]).astype(f32).reshape(-1))
    cols.append(seg.astype(f32))
    masks = jnp.pad(jnp.stack(cols, 1), ((0, PAD), (0, 2)))
    segr = grid.astype(f32)
    rates = jnp.stack([mine(dt_bias, 0, heads), -jnp.exp(mine(a_log, 0, heads)), mine(d_skip, 0, heads)])
    rates = jnp.pad(jnp.repeat(rates, head, axis=1), ((0, 5), (0, 0)))

    cat = channels + bcw
    front = call(
        lambda *r: front_kernel(dims, *r),
        [idx, segr, masks, rates, own] + tok_mine + tok_other + wa_parts + [bc_other],
        [
            ((total, width), bf16),
            ((width, cat + MISC), bf16),
            ((2 * MISC, channels), f32),
            ((total + PAD, cat), bf16),
            ((total, cat), f32),
            ((total, channels), f32),
            ((total, channels), f32),
            ((total // SPAN * channels, state), bf16),
        ],
        [((width, channels), bf16), ((channels, state), f32), ((total + PAD, cat), f32)],
    )
    normed, wfull, small, pre, uall, dtraw, ssd, states = front
    sums, cotfull, wzo, zval, dyn = call(
        lambda *r: gate_kernel(dims, *r),
        [idx, normed, ssd, small, cot] + cot_mine + cot_other + wb_parts,
        [
            ((2, total), f32),
            ((total, width), bf16),
            ((width, 2 * channels), bf16),
            ((total, channels), f32),
            ((total, channels), f32),
        ],
        [],
    )
    sums = sums + swap(sums, "tensor", 1)
    k = 1
    while k < contexts:
        sums = sums + swap(sums, "context", k)
        k *= 2
    part = width // 2
    mid = call(
        lambda *r: mid_kernel(dims, inner, *r),
        [idx, sums, normed, ssd, small, cotfull, wzo, zval, dyn],
        [
            ((total, part), bf16),
            ((total, part), bf16),
            ((total, channels), bf16),
            ((total, channels), f32),
            ((8, channels), f32),
        ]
        + [((rows, 2 * channels), bf16)] * shards,
        [((total, channels), bf16)],
    )
    okeep, osend, dz, dssd, ogg = mid[:5]
    zo = mid[5:]

    def stream_reduce(keep, send):
        full = keep.astype(f32) + swap(send, "tensor", 1).astype(f32)

        def rows_of(k):
            return lax.dynamic_slice_in_dim(full, (c ^ k) * length, length, 0)

        got = [swap(rows_of(k).astype(bf16), "context", k) for k in range(1, contexts)]
        return rows_of(0) + sum(g.astype(f32) for g in got)

    def shard_reduce(parts):
        got = [swap(parts[k], "shard", k) for k in range(1, shards)]
        return (parts[0].astype(f32) + sum(g.astype(f32) for g in got)).astype(bf16)

    def context_gather(x):
        return ordered([x] + [swap(x, "context", k) for k in range(1, contexts)], c)

    mixed = stream_reduce(okeep, osend)
    residual = lax.dynamic_slice_in_dim(own, t * part, part, 1).astype(f32)
    block_out = (residual + mixed).astype(bf16)[None]
    zo_all = context_gather(shard_reduce(zo))

    dkeep, dsend, gkeep, gsend = call(
        lambda *r: back_kernel(dims, *r),
        [idx, segr, masks, rates, normed, wfull, small, pre, uall, dtraw, ssd, states, wzo, dz, dssd, ogg],
        [
            ((total, part), bf16),
            ((total, part), bf16),
            ((width, channels + state + MISC), bf16),
            ((width, state + MISC), bf16),
        ],
        [
            ((total, cat + MISC), bf16),
            ((channels, state), f32),
            ((24, channels), f32),
        ],
    )
    lane = jnp.arange(MISC)
    common = (lane == GAIN) | ((lane >= BCP) & (lane < BCP + 5))
    grecv = swap(gsend, "tensor", 1).astype(f32)
    grecv = jnp.concatenate([grecv[:, :state], jnp.where(common, grecv[:, state:], 0.0)], 1)
    gfull = gkeep.astype(f32) + jnp.pad(grecv, ((0, 0), (channels, 0)))
    gparts = [
        lax.dynamic_slice_in_dim(gfull, (s ^ k) * rows, rows, 0).astype(bf16) for k in range(shards)
    ]
    fx = context_gather(shard_reduce(gparts))
    dpart = stream_reduce(dkeep, dsend).astype(bf16)
    dother = swap(dpart, "tensor", 1)
    dnormed = jnp.concatenate(
        [jnp.where(t == 0, dpart, dother), jnp.where(t == 0, dother, dpart)], 1
    ).astype(f32)

    xfloat = own.astype(f32)
    gain_full = wfull[:, cat + GAIN].astype(f32)
    rstd = lax.rsqrt(jnp.mean(xfloat * xfloat, -1, keepdims=True) + eps)
    weighted = dnormed * gain_full
    dx = rstd * weighted - xfloat * rstd**3 * jnp.mean(weighted * xfloat, -1, keepdims=True)
    tokens_grad = (cot.astype(f32) + dx)[None]

    inproj_grad = jnp.concatenate(
        [p[:, None, 0:channels] for p in zo_all], 2
    )
    inproj_grad = jnp.concatenate(
        [inproj_grad, jnp.concatenate([p[:, None, 0:channels] for p in fx], 2)], 1
    ).astype(f32)
    outproj_grad = jnp.concatenate([p[:, channels:].T for p in zo_all], 0).astype(f32)
    shared = sum(p[:, channels:].astype(f32) for p in fx)
    bc_half = shared[:, :state].astype(bf16)
    bc_away = swap(bc_half, "tensor", 1)
    bcproj_grad = jnp.concatenate(
        [jnp.where(t == 0, bc_half, bc_away), jnp.where(t == 0, bc_away, bc_half)], 1
    ).astype(f32)
    shared = shared[:, state:]
    miscs = [p[:, channels + state :].astype(f32) for p in fx]
    dtproj_grad = jnp.concatenate([m[:, 0:heads] for m in miscs], 1)
    normgain_grad = shared[:, GAIN]
    piece = head // shards
    headg = jnp.stack([m[: heads * piece, HEADP : HEADP + 6] for m in miscs])
    headg = headg.reshape(contexts * heads, piece, 6)
    convw_grad = jnp.transpose(headg[:, :, 0:CONV], (2, 0, 1))
    convb_grad = headg[:, :, CONV]
    outgain_grad = headg[:, :, CONV + 1]
    bcg = shared[: bcw // shards, BCP : BCP + 5]
    bcconv_grad = bcg[:, 0:CONV].T
    bcbias_grad = bcg[:, CONV]
    small_rates = jnp.concatenate([m[0:heads, RATE : RATE + 3] for m in miscs], 0)
    return (
        block_out,
        tokens_grad,
        normgain_grad,
        inproj_grad,
        bcproj_grad,
        dtproj_grad,
        convw_grad,
        convb_grad,
        bcconv_grad,
        bcbias_grad,
        small_rates[:, 0],
        small_rates[:, 1],
        small_rates[:, 2],
        outgain_grad,
        outproj_grad,
    )


def solution(mesh):
    return jax.shard_map(
        on_device,
        mesh=mesh,
        in_specs=(
            P("shard", "context", None),
            P("shard", None),
            P("shard"),
            P("shard", None, "tensor"),
            P("shard", None),
            P("shard", "tensor"),
            P(None, "tensor", "shard"),
            P("tensor", "shard"),
            P(None, "shard"),
            P("shard"),
            P("tensor"),
            P("tensor"),
            P("tensor"),
            P("tensor", "shard"),
            P("tensor", "shard"),
            P("shard", "context", None),
        ),
        out_specs=(
            P("shard", "context", "tensor"),
            P("shard", "context", None),
            P("shard"),
            P("shard", None, "tensor"),
            P("shard", None),
            P("shard", "tensor"),
            P(None, "tensor", "shard"),
            P("tensor", "shard"),
            P(None, "shard"),
            P("shard"),
            P("tensor"),
            P("tensor"),
            P("tensor"),
            P("tensor", "shard"),
            P("tensor", "shard"),
        ),
        check_vma=False,
    )
```

```python
import jax
import jax.numpy as jnp
from jax import lax
from jax.experimental import pallas as pl
from jax.experimental.pallas import tpu as pltpu
from jax.sharding import PartitionSpec as P

CONV = 4
SPAN = 128
PAD = 16
GAIN = 8
HEADP = 16
BCP = 24
RATE = 40
BCLO = 32
MISC = 128
eps = 1e-05
f32 = jnp.float32
bf16 = jnp.bfloat16


def mm(a, b, ca=1, cb=0):
    return lax.dot_general(a, b, (((ca,), (cb,)), ((), ())), preferred_element_type=f32)


def pieces(x, count):
    parts = []
    for _ in range(count):
        part = x.astype(bf16)
        parts.append(part)
        x = x - part.astype(f32)
    return parts


def mm3(a, b, ca=1, cb=0):
    ah, al = pieces(a, 2)
    bh, bl = pieces(b, 2)
    return mm(ah, bh, ca, cb) + (mm(al, bh, ca, cb) + mm(ah, bl, ca, cb))


def exact_left(ones, x, count, cb=0):
    return sum(mm(ones, part, 1, cb) for part in pieces(x, count))


def exact_right(x, ones, count, ca=1, cb=0):
    return sum(mm(part, ones, ca, cb) for part in pieces(x, count))


def iota(shape, dim):
    return lax.broadcasted_iota(jnp.int32, shape, dim)


def low(x, size):
    return lax.bitwise_and(x, jnp.int32(size - 1))


def high(x, size):
    return lax.shift_right_logical(x, jnp.int32(size.bit_length() - 1))


def sigmoid(x):
    return 1.0 / (1.0 + jnp.exp(-x))


def softplus(x):
    return jnp.maximum(x, 0.0) + jnp.log1p(jnp.exp(-jnp.abs(x)))


def spread_head(width, shards, channels, head):
    rows = width // shards
    part = head // shards
    used = (channels // head) * part
    r, c = iota((width, channels), 0), iota((width, channels), 1)
    s, q = high(r, rows), low(r, rows)
    hit = (c == high(q, part) * head + s * part + low(q, part)) & (q < used)
    return hit.astype(f32).astype(bf16)


def spread_bc(width, shards, channels):
    rows = width // shards
    part = channels // shards
    r, c = iota((width, channels), 0), iota((width, channels), 1)
    s, q = high(r, rows), low(r, rows)
    return ((c == s * part + q) & (q < part)).astype(f32).astype(bf16)


def spread_rate(width, shards, channels, head):
    rows = width // shards
    r, c = iota((width, channels), 0), iota((width, channels), 1)
    q = low(r, rows)
    return ((c == q * head) & (q < channels // head)).astype(f32).astype(bf16)


def block_ones(channels, head):
    r, c = iota((channels, channels), 0), iota((channels, channels), 1)
    return (high(r, head) == high(c, head)).astype(f32).astype(bf16)


def one_hot(rows, cols, row, col):
    return ((iota((rows, cols), 0) == row) & (iota((rows, cols), 1) == col)).astype(f32).astype(bf16)


def triangle(lower):
    r, c = iota((SPAN, SPAN), 0), iota((SPAN, SPAN), 1)
    hit = (r >= c) if lower else (r <= c)
    return hit.astype(f32).astype(bf16)


def local_decay(keep, a, at, head, h):
    diff = a[:, h * head : h * head + 1] - at[h * head : h * head + 1, :]
    return jnp.exp(jnp.where(keep, diff, -1e30))


def front_kernel(dims, *refs):
    shards, contexts, head, channels, state = dims
    it = iter(refs)
    idx = next(it)
    segr, masks, rates = next(it), next(it), next(it)
    own = next(it)
    mine = [next(it) for _ in range(contexts - 1)]
    other = [next(it) for _ in range(contexts - 1)]
    wparts = [next(it) for _ in range(shards)]
    mparts = [next(it) for _ in range(shards)]
    bcother = next(it)
    cown = next(it)
    cmine = [next(it) for _ in range(contexts - 1)]
    cother = [next(it) for _ in range(contexts - 1)]
    normed, wfull, small, pre, uall, dtraw, ssd, states, cot = (next(it) for _ in range(9))
    wdt, sref, pref = (next(it) for _ in range(3))
    c, t, s = idx[0], idx[1], idx[2]
    length, width = own.shape
    half = length // 2
    total = length * contexts
    rows = width // shards
    bcw = 2 * state
    for k in range(shards):
        at = pl.multiple_of((s ^ k) * rows, rows)
        part = mparts[k]
        wfull[pl.ds(at, rows), 0:channels] = wparts[k][...]
        here, there = part[:, 0:state], bcother[k]
        wfull[pl.ds(at, rows), channels : channels + state] = jnp.where(t == 0, here, there)
        wfull[pl.ds(at, rows), channels + state : channels + bcw] = jnp.where(t == 0, there, here)
        wfull[pl.ds(at, rows), channels + bcw :] = part[:, state:]
    assemble_tokens(cot, idx, cown, cmine, cother)
    misc = wfull[:, channels + bcw :]
    small[0:MISC, :] = mm(misc, spread_head(width, shards, channels, head), 0, 0)
    small[MISC:, :] = mm(misc, spread_bc(width, shards, bcw), 0, 0)
    expand = (iota((MISC, channels), 0) == high(iota((MISC, channels), 1), head)).astype(f32)
    wdt[...] = mm(misc, expand.astype(bf16)).astype(bf16)
    gain = mm(one_hot(8, MISC, 0, GAIN), misc, 1, 1)[0:1, :]

    def norm(tokens):
        x = tokens.astype(f32)
        return (x * lax.rsqrt(jnp.mean(x * x, -1, keepdims=True) + eps) * gain).astype(bf16)

    for q in range(length // SPAN):
        normed[pl.ds(pl.multiple_of(c * length + q * SPAN, SPAN), SPAN), :] = norm(
            own[q * SPAN : (q + 1) * SPAN, :]
        )
    for k in range(1, contexts):
        base = (c ^ k) * length
        normed[pl.ds(pl.multiple_of(base + t * half, half), half), :] = norm(mine[k - 1][...])
        normed[pl.ds(pl.multiple_of(base + (1 - t) * half, half), half), :] = norm(other[k - 1][...])
    pref[0:PAD, :] = jnp.zeros((PAD, channels + bcw), f32)
    pre[0:PAD, :] = jnp.zeros((PAD, channels + bcw), bf16)
    chunk = 2 * SPAN

    def project(i, _):
        at = pl.multiple_of(i * chunk, chunk)
        n = normed[pl.ds(at, chunk), :]
        value = mm(n, wfull[:, 0 : channels + bcw]).astype(bf16)
        pre[pl.ds(pl.multiple_of(at + PAD, PAD), chunk), :] = value
        pref[pl.ds(pl.multiple_of(at + PAD, PAD), chunk), :] = value.astype(f32)
        dtraw[pl.ds(at, chunk), :] = mm(n, wdt[...])
        return 0

    lax.fori_loop(0, total // chunk, project, 0)
    sref[...] = jnp.zeros_like(sref)
    tri = triangle(True)
    causal = iota((SPAN, SPAN), 0) >= iota((SPAN, SPAN), 1)
    side = iota((SPAN, 2 * head), 1) < head

    def scan(i, _):
        at = pl.multiple_of(i * SPAN, SPAN)
        window = pref[pl.ds(at, SPAN + PAD), :]
        mk = masks[pl.ds(at, SPAN), :]
        taps = jnp.concatenate(
            [small[HEADP : HEADP + 8, :], small[MISC + BCP : MISC + BCP + 8, :]], 1
        )
        u = taps[CONV - 1 : CONV, :] * window[PAD:, :]
        bias = jnp.concatenate(
            [small[HEADP + 4 : HEADP + 5, :], small[MISC + BCP + 4 : MISC + BCP + 5, :]], 1
        )
        u = u + bias
        for j in range(1, CONV):
            u = u + taps[CONV - 1 - j : CONV - j, :] * (
                window[PAD - j : PAD - j + SPAN, :] * mk[:, j - 1 : j]
            )
        uall[pl.ds(at, SPAN), :] = u
        act = u * sigmoid(u)
        x = act[:, 0:channels]
        bfull, cfull = act[:, channels : channels + state], act[:, channels + state :]
        bb, cb = bfull.astype(bf16), cfull.astype(bf16)
        dt = softplus(dtraw[pl.ds(at, SPAN), :] + rates[0:1, :])
        a = exact_left(tri, rates[1:2, :] * dt, 3)
        att = a.T
        step = x * dt
        ub = step.astype(bf16)
        g = mm3(cfull, bfull, 1, 1)
        keep = (mk[:, 5:6] == segr[pl.ds(i, 1), :]) & causal
        inner = []
        for pair in range(channels // (2 * head)):
            up = ub[:, pair * 2 * head : (pair + 1) * 2 * head]
            both = [
                mm((g * local_decay(keep, a, att, head, 2 * pair + e)).astype(bf16), up)
                for e in range(2)
            ]
            inner.append(jnp.where(side, both[0], both[1]))
        before = sref[...]
        sb = before.astype(bf16)
        states[pl.ds(pl.multiple_of(i * channels, channels), channels), :] = sb
        carry = jnp.exp(a) * mk[:, 3:4]
        y = jnp.concatenate(inner, 1) + carry * mm(cb, sb, 1, 1)
        ssd[pl.ds(at, SPAN), :] = y + rates[2:3, :] * x
        tail = jnp.exp(a[SPAN - 1 :, :] - a) * mk[:, 4:5]
        through = jnp.exp(att[:, SPAN - 1 :]) * mk[SPAN - 1 :, 3:4]
        sref[...] = through * before + mm((tail * step).astype(bf16), bb, 0, 0)
        return 0

    lax.fori_loop(0, total // SPAN, scan, 0)


def assemble_tokens(dst, idx, own, mine, other):
    c, t = idx[0], idx[1]
    length = own.shape[0]
    half = length // 2
    dst[pl.ds(pl.multiple_of(c * length, length), length), :] = own[...]
    for k in range(1, len(mine) + 1):
        base = (c ^ k) * length
        dst[pl.ds(pl.multiple_of(base + t * half, half), half), :] = mine[k - 1][...]
        dst[pl.ds(pl.multiple_of(base + (1 - t) * half, half), half), :] = other[k - 1][...]


def gate_kernel(dims, *refs):
    shards, _, _, channels, _ = dims
    it = iter(refs)
    idx = next(it)
    normed, ssd, small, cot = next(it), next(it), next(it), next(it)
    wparts = [next(it) for _ in range(shards)]
    sums, wzo, zval, dyn = (next(it) for _ in range(4))
    s = idx[2]
    width = normed.shape[1]
    rows = width // shards
    for k in range(shards):
        wzo[pl.ds(pl.multiple_of((s ^ k) * rows, rows), rows), :] = wparts[k][...]
    chunk = 2 * SPAN
    ogain = small[HEADP + 5 : HEADP + 6, :]
    ones = jnp.ones((8, channels), bf16)
    for i in range(normed.shape[0] // chunk):
        at = slice(i * chunk, (i + 1) * chunk)
        z = mm(normed[at, :], wzo[:, 0:channels])
        d = mm(cot[at, :], wzo[:, channels:])
        zval[at, :] = z
        dyn[at, :] = d
        gated = ssd[at, :] * (z * sigmoid(z))
        sums[0:1, at] = exact_left(ones, gated * gated, 2, 1)[0:1, :]
        sums[1:2, at] = exact_left(ones, d * ogain * gated, 2, 1)[0:1, :]


def mid_kernel(dims, inner, *refs):
    shards, _, _, channels, _ = dims
    it = iter(refs)
    idx = next(it)
    sums, normed, ssd, small, cot, wzo, zval, dyn = (next(it) for _ in range(8))
    okeep, osend, dz, dssd, ogg, ngz = (next(it) for _ in range(6))
    gparts = [next(it) for _ in range(shards)]
    yref = next(it)
    t, s = idx[1], idx[2]
    total, width = normed.shape
    rows = width // shards
    part = width // 2
    chunk = 2 * SPAN
    ogain = small[HEADP + 5 : HEADP + 6, :]
    first = (iota((8, channels), 0) == 0).astype(f32).astype(bf16)
    second = (iota((8, channels), 0) == 1).astype(f32).astype(bf16)
    gacc = jnp.zeros((1, channels), f32)
    keep_at = pl.multiple_of(t * part, part)
    send_at = pl.multiple_of((1 - t) * part, part)
    for i in range(total // chunk):
        at = slice(i * chunk, (i + 1) * chunk)
        pair = jnp.concatenate([sums[:, at], jnp.zeros((6, chunk), f32)], 0)
        square = exact_right(pair, first, 3, 0, 0)
        cross = exact_right(pair, second, 3, 0, 0)
        z = zval[at, :]
        sg = sigmoid(z)
        zs = z * sg
        out = ssd[at, :]
        gated = out * zs
        r = lax.rsqrt(square / inner + eps)
        ynorm = (gated * r * ogain).astype(bf16)
        yref[at, :] = ynorm
        okeep[at, :] = mm(ynorm, wzo[pl.ds(keep_at, part), channels:], 1, 1).astype(bf16)
        osend[at, :] = mm(ynorm, wzo[pl.ds(send_at, part), channels:], 1, 1).astype(bf16)
        d = dyn[at, :]
        dgated = r * (d * ogain) - gated * (r * r * r) * (cross / inner)
        dssd[at, :] = dgated * zs
        dz[at, :] = (dgated * out * (sg * (1.0 + z * (1.0 - sg)))).astype(bf16)
        gacc = gacc + jnp.sum(d * gated * r, 0, keepdims=True)
    ogg[...] = jnp.broadcast_to(gacc, ogg.shape)
    for k in range(shards):
        at = pl.multiple_of((s ^ k) * rows, MISC)
        gz = mm(normed[:, pl.ds(at, rows)], dz[...], 0, 0)
        wrows = pl.ds(pl.multiple_of((s ^ k) * rows, rows), rows)
        dots = jnp.sum(gz * wzo[wrows, 0:channels].astype(f32), -1, keepdims=True)
        ngz[wrows, :] = jnp.broadcast_to(dots, (rows, MISC))
        gparts[k][:, 0:channels] = gz.astype(bf16)
        gparts[k][:, channels:] = mm(cot[:, pl.ds(at, rows)], yref[...], 0, 0).astype(bf16)


def scan_kernel(dims, *refs):
    _, _, head, channels, state = dims
    it = iter(refs)
    idx = next(it)
    segr, masks, rates = next(it), next(it), next(it)
    small, pre, uall, dtraw, ssd, states, dssd = (next(it) for _ in range(7))
    dcat, acc, dsref = (next(it) for _ in range(3))
    total = uall.shape[0]
    bcw = 2 * state
    cat = channels + bcw
    blocks = total // SPAN
    dsref[...] = jnp.zeros_like(dsref)
    acc[...] = jnp.zeros_like(acc)
    lower, upper = triangle(True), triangle(False)
    ones = block_ones(channels, head)
    causal = iota((SPAN, SPAN), 0) >= iota((SPAN, SPAN), 1)
    side = iota((SPAN, 2 * head), 1) < head
    last = iota((SPAN, channels), 0) == SPAN - 1
    sel = (
        iota((channels, MISC), 0) == iota((channels, MISC), 1) * head
    ).astype(f32).astype(bf16)
    row8 = jnp.ones((8, state), bf16)

    def step(ii, halo):
        i = blocks - 1 - ii
        at = pl.multiple_of(i * SPAN, SPAN)
        here = pl.ds(at, SPAN)
        mk = masks[pl.ds(at, SPAN + PAD), :]
        mh = mk[0:SPAN, :]
        u = uall[here, :]
        sg = sigmoid(u)
        act = u * sg
        x = act[:, 0:channels]
        bfull, cfull = act[:, channels : channels + state], act[:, channels + state :]
        bb, cb = bfull.astype(bf16), cfull.astype(bf16)
        raw = dtraw[here, :] + rates[0:1, :]
        dt = softplus(raw)
        dec = rates[1:2, :] * dt
        a = exact_left(lower, dec, 3)
        att = a.T
        us = x * dt
        ub = us.astype(bf16)
        dy = dssd[here, :]
        dyb = dy.astype(bf16)
        g = mm3(cfull, bfull, 1, 1)
        keep = (mh[:, 5:6] == segr[pl.ds(i, 1), :]) & causal
        carry = jnp.exp(a) * mh[:, 3:4]
        tail = jnp.exp(a[SPAN - 1 :, :] - a) * mh[:, 4:5]
        sb = states[pl.ds(pl.multiple_of(i * channels, channels), channels), :]
        nxt = jnp.minimum(i + 1, blocks - 1)
        snext = states[pl.ds(pl.multiple_of(nxt * channels, channels), channels), :].astype(f32)
        dsn = dsref[...]
        dsb = dsn.astype(bf16)
        cdy = carry * dy
        tu = tail * us
        dg = jnp.zeros((SPAN, SPAN), f32)
        dus = []
        for pair in range(channels // (2 * head)):
            lanes = slice(pair * 2 * head, (pair + 1) * 2 * head)
            dyp = dyb[:, lanes]
            both = []
            for e in range(2):
                decay = local_decay(keep, a, att, head, 2 * pair + e)
                mine = side if e == 0 else jnp.logical_not(side)
                dm = mm3(dy[:, lanes], jnp.where(mine, us[:, lanes], 0.0), 1, 1)
                dg = dg + dm * decay
                both.append(mm((g * decay).astype(bf16), dyp, 0, 0))
            dus.append(jnp.where(side, both[0], both[1]))
        dc = mm3(dg, bfull) + exact_right(cdy, sb, 2)
        db = mm3(dg, cfull, 0, 0) + mm3(tu, dsn)
        du = jnp.concatenate(dus, 1) + tail * mm(bb, dsb, 1, 1)
        through = jnp.exp(att[:, SPAN - 1 :]) * mh[SPAN - 1 :, 3:4]
        dsref[...] = through * dsn + mm(cdy.astype(bf16), cb, 0, 0)
        y = ssd[here, :] - rates[2:3, :] * x
        extra = exact_left(row8, snext * dsn, 3, 1)[0:1, :]
        e = dyb.astype(f32) * y - ub.astype(f32) * du
        e = e + jnp.where(last, extra, 0.0)
        ddec = exact_right(exact_left(upper, e, 3), ones, 3)
        xdu = exact_right(x * du, ones, 2)
        ddt = (xdu + rates[1:2, :] * ddec) * sigmoid(raw)
        acc[8:9, :] = acc[8:9, :] + jnp.sum(ddt, 0, keepdims=True)
        acc[9:10, :] = acc[9:10, :] + jnp.sum(ddec * dec, 0, keepdims=True)
        acc[10:11, :] = acc[10:11, :] + jnp.sum(dy * x, 0, keepdims=True)
        dx = dt * du + rates[2:3, :] * dy
        dact = jnp.concatenate([dx, db, dc], 1)
        dut = dact * (sg * (1.0 + u * (1.0 - sg)))
        dwin = jnp.concatenate([dut, halo], 0)
        pwin = pre[pl.ds(at, SPAN + PAD), :].astype(f32)
        taps = jnp.concatenate(
            [small[HEADP : HEADP + 8, :], small[MISC + BCP : MISC + BCP + 8, :]], 1
        )
        dpre = taps[CONV - 1 : CONV, :] * dut

        def gather(row, value):
            total_row = jnp.sum(value, 0, keepdims=True)
            acc[row : row + 1, :] = acc[row : row + 1, :] + total_row[:, 0:channels]
            acc[16 + row : 17 + row, 0:bcw] = acc[16 + row : 17 + row, 0:bcw] + total_row[:, channels:]

        gather(CONV - 1, dut * pwin[PAD:, :])
        gather(CONV, dut)
        for j in range(1, CONV):
            moved = dwin * mk[:, j - 1 : j]
            dpre = dpre + taps[CONV - 1 - j : CONV - j, :] * moved[j : j + SPAN, :]
            gather(CONV - 1 - j, moved[0:SPAN, :] * pwin[PAD - j : PAD - j + SPAN, :])
        dcat[here, 0:cat] = dpre.astype(bf16)
        dcat[here, cat:] = mm(ddt.astype(bf16), sel).astype(bf16)
        return dut[0:PAD, :]

    lax.fori_loop(0, blocks, step, jnp.zeros((PAD, cat), f32))
    acc[8:16, :] = jnp.where(
        iota((8, channels), 0) == 2, exact_right(acc[8:16, :], ones, 3), acc[8:16, :]
    )


def token_kernel(dims, *refs):
    _, _, _, channels, _ = dims
    idx, wfull, wzo, dz, dcat, dkeep, dsend = refs
    t = idx[1]
    total, width = dcat.shape[0], wfull.shape[0]
    part = width // 2
    chunk = 2 * SPAN
    for i in range(total // chunk):
        at = slice(i * chunk, (i + 1) * chunk)
        full = mm(dcat[at, :], wfull[...], 1, 1) + mm(dz[at, :], wzo[:, 0:channels], 1, 1)
        lo, hi = full[:, 0:part].astype(bf16), full[:, part:].astype(bf16)
        dkeep[at, :] = jnp.where(t == 0, lo, hi)
        dsend[at, :] = jnp.where(t == 0, hi, lo)


def weight_kernel(dims, *refs):
    shards, _, head, channels, state = dims
    idx, normed, wfull, dcat, acc, ogg, ngz, gkeep, gsend = refs
    t = idx[1]
    width = wfull.shape[0]
    bcw = 2 * state
    cat = channels + bcw
    chunk = 2 * SPAN
    headg = jnp.where(iota((8, channels), 0) == 5, ogg[0:8, :], acc[0:8, :])
    z8 = jnp.zeros((8, channels), f32)

    def place(rowsets, spread):
        stack = [z8] * (MISC // 8)
        for row, value in rowsets:
            stack[row // 8] = value
        return mm(spread, jnp.concatenate(stack, 0).astype(bf16), 1, 1)

    misc = place([(HEADP, headg)], spread_head(width, shards, channels, head))
    bch, bcl = pieces(acc[16:24, 0:bcw], 2)
    misc = misc + place(
        [(BCP, bch.astype(f32)), (BCLO, bcl.astype(f32))], spread_bc(width, shards, bcw)
    )
    misc = misc + place([(RATE, acc[8:16, :])], spread_rate(width, shards, channels, head))
    gain_lane = (iota((1, MISC), 1) == GAIN).astype(f32)
    for i in range(width // chunk):
        at = slice(i * chunk, (i + 1) * chunk)
        gw = mm(normed[:, at], dcat[...], 0, 0)
        w = wfull[at, :].astype(f32)
        ng = jnp.sum(gw * w, -1, keepdims=True) + ngz[at, 0:1]
        ng = ng / w[:, cat + GAIN : cat + GAIN + 1]
        gkeep[at, 0:channels] = gw[:, 0:channels].astype(bf16)
        b, c = gw[:, channels : channels + state], gw[:, channels + state : cat]
        gkeep[at, channels : channels + state] = jnp.where(t == 0, b, c).astype(bf16)
        gsend[at, 0:state] = jnp.where(t == 0, c, b).astype(bf16)
        m = (gw[:, cat:] + misc[at, :] + ng * gain_lane).astype(bf16)
        gkeep[at, channels + state :] = m
        gsend[at, state:] = m


def outer_kernel(dims, *refs):
    _, contexts, _, channels, _ = dims
    idx, parts, out = refs[0], refs[1:-1], refs[-1]
    for k in range(contexts):
        at = pl.multiple_of((idx[0] ^ k) * channels, channels)
        out[pl.ds(at, channels), :] = parts[k][:, channels:].astype(f32).T


def final_kernel(dims, *refs):
    shards, contexts, head, channels, state = dims
    idx = refs[0]
    zparts, xparts = refs[1 : 1 + contexts], refs[1 + contexts : 1 + 2 * contexts]
    gi, dt, ng, cw, cb, og, bcc, bcb, ra, rb, rc = refs[1 + 2 * contexts :]
    c = idx[0]
    rows = gi.shape[0]
    heads = channels // head
    piece = head // shards
    span = heads * piece
    every = contexts * span
    names = contexts * heads
    pick = iota((8, MISC), 1)
    line = iota((8, MISC), 0)
    bcsel = ((pick == line + BCP) | (pick == line + BCLO)) & (line < 5)
    bcsel = bcsel.astype(f32).astype(bf16)
    gsel = one_hot(8, MISC, 0, GAIN)
    dts = jnp.zeros((rows, names), f32)
    gains = jnp.zeros((8, rows), f32)
    bcs = jnp.zeros((8, rows), f32)
    small = jnp.zeros((MISC, every), f32)
    rates = jnp.zeros((MISC, names), f32)
    for k in range(contexts):
        place = c ^ k
        at = pl.multiple_of(place * channels, channels)
        gi[:, 0, pl.ds(at, channels)] = zparts[k][:, 0:channels].astype(f32)
        gi[:, 1, pl.ds(at, channels)] = xparts[k][:, 0:channels].astype(f32)
        m = xparts[k][:, channels + state :]

        def to_lane(count, width, size):
            r, q = iota((count, width), 0), iota((count, width), 1)
            return ((q == place * size + r) & (r < size)).astype(f32).astype(bf16)

        dts = dts + mm(m, to_lane(MISC, names, heads))
        gains = gains + mm(gsel, m, 1, 1)
        bcs = bcs + mm(bcsel, m, 1, 1)
        small = small + mm(m, to_lane(rows, every, span), 0, 0)
        rates = rates + mm(m, to_lane(rows, names, heads), 0, 0)
    dt[...] = dts
    ng[...] = gains[0:1, :]
    bcc[...] = bcs[0:CONV, 0 : bcc.shape[1]]
    bcb[...] = bcs[CONV : CONV + 1, 0 : bcb.shape[1]]
    mine = high(iota((names, every), 1), piece) == iota((names, every), 0)
    fold = (low(iota((every, piece), 0), piece) == iota((every, piece), 1)).astype(f32).astype(bf16)

    def split(row):
        return mm(jnp.where(mine, small[row : row + 1, :], 0.0).astype(bf16), fold)

    for j in range(CONV):
        cw[j] = split(HEADP + j)
    cb[...] = split(HEADP + CONV)
    og[...] = split(HEADP + CONV + 1)
    for j, ref in enumerate((ra, rb, rc)):
        ref[...] = rates[RATE + j : RATE + j + 1, :]


def swap(x, axis, k):
    return lax.ppermute(x, axis, [(i, i ^ k) for i in range(lax.axis_size(axis))])


def call(cost, body, args, outs, scratch):
    smem = pl.BlockSpec(memory_space=pltpu.SMEM)
    vmem = pl.BlockSpec(memory_space=pltpu.VMEM)
    return launch(cost, body, args, outs, scratch, smem, vmem)


def launch(cost, body, args, outs, scratch, smem, vmem):
    return pl.pallas_call(
        body,
        cost_estimate=pl.CostEstimate(flops=cost * 10**9, transcendentals=0, bytes_accessed=1 << 20),
        out_shape=[jax.ShapeDtypeStruct(s, d) for s, d in outs],
        in_specs=[smem] + [vmem] * (len(args) - 1),
        out_specs=[vmem] * len(outs),
        scratch_shapes=[pltpu.VMEM(s, d) for s, d in scratch],
        compiler_params=pltpu.CompilerParams(vmem_limit_bytes=56 << 20),
    )(*args)


def stream_parts(rows, core, contexts):
    half = rows.shape[0] // 2
    mine = lax.dynamic_slice_in_dim(rows, core * half, half, 0)
    return [swap(mine, "context", k) for k in range(1, contexts)]


def layer(
    tokens,
    segment_ids,
    norm_gain,
    in_proj,
    bc_proj,
    dt_proj,
    conv_weight,
    conv_bias,
    bc_conv,
    bc_bias,
    dt_bias,
    a_log,
    d_skip,
    out_gain,
    out_proj,
    cotangent,
):
    shards, contexts = lax.axis_size("shard"), lax.axis_size("context")
    s, c, t = lax.axis_index("shard"), lax.axis_index("context"), lax.axis_index("tensor")
    idx = jnp.stack([c, t, s]).astype(jnp.int32)
    length, width = tokens.shape[1:]
    total = length * contexts
    rows = in_proj.shape[0]
    heads = dt_bias.shape[0] // contexts
    state = bc_proj.shape[1] // 2
    bcw = 2 * state
    channels = in_proj.shape[2] // contexts
    head = channels // heads
    inner = in_proj.shape[2] * lax.axis_size("tensor")
    dims = (shards, contexts, head, channels, state)
    own, cot = tokens[0], cotangent[0]

    def mine(x, dim, size):
        return lax.dynamic_slice_in_dim(x, c * size, size, dim)

    tok_mine = stream_parts(own, t, contexts)
    both = lax.dynamic_slice(in_proj, (0, 0, c * channels), (rows, 2, channels))
    hparts = [
        mine(conv_weight, 1, heads).reshape(CONV, -1),
        mine(conv_bias, 0, heads).reshape(1, -1),
        mine(out_gain, 0, heads).reshape(1, -1),
    ]
    headp = jnp.concatenate(hparts, 0).T
    bcp = jnp.concatenate([bc_conv, bc_bias[None]], 0).T

    def column(x, at):
        return jnp.pad(x, ((0, rows - x.shape[0]), (at, MISC - at - x.shape[1])))

    misc = (
        column(mine(dt_proj, 1, heads), 0)
        + column(norm_gain[:, None], GAIN)
        + column(headp, HEADP)
        + column(bcp, BCP)
    )
    wx = both[:, 1]
    wx_parts = [wx] + [swap(wx, "shard", k) for k in range(1, shards)]
    wm = jnp.concatenate([lax.dynamic_slice_in_dim(bc_proj, t * state, state, 1), misc], 1)
    wm_parts = [wm] + [swap(wm, "shard", k) for k in range(1, shards)]
    bc_other = swap(jnp.stack([w[:, :state] for w in wm_parts]), "tensor", 1)
    tok_other = [swap(x, "tensor", 1) for x in tok_mine]
    cot_mine = stream_parts(cot, t, contexts)
    wo = mine(out_proj, 0, channels).T
    wb = jnp.concatenate([both[:, 0], wo], 1)
    wb_parts = [wb] + [swap(wb, "shard", k) for k in range(1, shards)]
    cot_other = [swap(x, "tensor", 1) for x in cot_mine]

    seg = segment_ids[0]
    cols = []
    for j in range(1, CONV):
        moved = jnp.concatenate([jnp.full((j,), -1, jnp.int32), seg[:-j]])
        cols.append((moved == seg).astype(f32))
    grid = seg.reshape(total // SPAN, SPAN)
    previous = jnp.concatenate([jnp.full((1,), -1, jnp.int32), grid[:-1, -1]])
    cols.append((grid == previous[:, None]).astype(f32).reshape(-1))
    cols.append((grid == grid[:, -1:]).astype(f32).reshape(-1))
    cols.append(seg.astype(f32))
    masks = jnp.pad(jnp.stack(cols, 1), ((0, PAD), (0, 2)))
    segr = grid.astype(f32)
    rates = jnp.stack([mine(dt_bias, 0, heads), -jnp.exp(mine(a_log, 0, heads)), mine(d_skip, 0, heads)])
    rates = jnp.pad(jnp.repeat(rates, head, axis=1), ((0, 5), (0, 0)))

    cat = channels + bcw
    front = call(
        15,
        lambda *r: front_kernel(dims, *r),
        [idx, segr, masks, rates, own]
        + tok_mine
        + tok_other
        + wx_parts
        + wm_parts
        + [bc_other, cot]
        + cot_mine
        + cot_other,
        [
            ((total, width), bf16),
            ((width, cat + MISC), bf16),
            ((2 * MISC, channels), f32),
            ((total + PAD, cat), bf16),
            ((total, cat), f32),
            ((total, channels), f32),
            ((total, channels), f32),
            ((total // SPAN * channels, state), bf16),
            ((total, width), bf16),
        ],
        [((width, channels), bf16), ((channels, state), f32), ((total + PAD, cat), f32)],
    )
    normed, wfull, small, pre, uall, dtraw, ssd, states, cotfull = front
    sums, wzo, zval, dyn = call(
        7,
        lambda *r: gate_kernel(dims, *r),
        [idx, normed, ssd, small, cotfull] + wb_parts,
        [
            ((2, total), f32),
            ((width, 2 * channels), bf16),
            ((total, channels), f32),
            ((total, channels), f32),
        ],
        [],
    )
    sums = sums + swap(sums, "tensor", 1)
    k = 1
    while k < contexts:
        sums = sums + swap(sums, "context", k)
        k *= 2
    part = width // 2
    mid = call(
        8,
        lambda *r: mid_kernel(dims, inner, *r),
        [idx, sums, normed, ssd, small, cotfull, wzo, zval, dyn],
        [
            ((total, part), bf16),
            ((total, part), bf16),
            ((total, channels), bf16),
            ((total, channels), f32),
            ((8, channels), f32),
            ((width, MISC), f32),
        ]
        + [((rows, 2 * channels), bf16)] * shards,
        [((total, channels), bf16)],
    )
    okeep, osend, dz, dssd, ogg, ngz = mid[:6]
    zo = mid[6:]

    def stream_reduce(keep, send):
        away = swap(send, "tensor", 1)
        full = keep.astype(f32) + away.astype(f32)

        def rows_of(k):
            return lax.dynamic_slice_in_dim(full, (c ^ k) * length, length, 0)

        got = [swap(rows_of(k).astype(bf16), "context", k) for k in range(1, contexts)]
        return rows_of(0) + sum(g.astype(f32) for g in got)

    def shard_reduce(parts):
        got = [swap(parts[k], "shard", k) for k in range(1, shards)]
        return (parts[0].astype(f32) + sum(g.astype(f32) for g in got)).astype(bf16)

    def context_gather(x):
        return [x] + [swap(x, "context", k) for k in range(1, contexts)]

    mixed = stream_reduce(okeep, osend)
    residual = lax.dynamic_slice_in_dim(own, t * part, part, 1).astype(f32)
    block_out = (residual + mixed).astype(bf16)[None]
    zo_all = context_gather(shard_reduce(zo))

    dcat, acc = call(
        22,
        lambda *r: scan_kernel(dims, *r),
        [idx, segr, masks, rates, small, pre, uall, dtraw, ssd, states, dssd],
        [((total, cat + MISC), bf16), ((24, channels), f32)],
        [((channels, state), f32)],
    )
    gkeep, gsend = call(
        4,
        lambda *r: weight_kernel(dims, *r),
        [idx, normed, wfull, dcat, acc, ogg, ngz],
        [((width, channels + state + MISC), bf16), ((width, state + MISC), bf16)],
        [],
    )
    dkeep, dsend = call(
        4,
        lambda *r: token_kernel(dims, *r),
        [idx, wfull, wzo, dz, dcat],
        [((total, part), bf16), ((total, part), bf16)],
        [],
    )
    lane = jnp.arange(MISC)
    common = (lane == GAIN) | ((lane >= BCP) & (lane < BCLO + 8))
    grecv = swap(gsend, "tensor", 1).astype(f32)
    grecv = jnp.concatenate([grecv[:, :state], jnp.where(common, grecv[:, state:], 0.0)], 1)
    gfull = gkeep.astype(f32) + jnp.pad(grecv, ((0, 0), (channels, 0)))
    gparts = [
        lax.dynamic_slice_in_dim(gfull, (s ^ k) * rows, rows, 0).astype(bf16) for k in range(shards)
    ]
    fx = context_gather(shard_reduce(gparts))
    dpart = stream_reduce(dkeep, dsend)
    dpart = dpart.astype(bf16)
    dother = swap(dpart, "tensor", 1)
    dnormed = jnp.concatenate(
        [jnp.where(t == 0, dpart, dother), jnp.where(t == 0, dother, dpart)], 1
    ).astype(f32)

    xfloat = own.astype(f32)
    gain_full = wfull[:, cat + GAIN].astype(f32)
    rstd = lax.rsqrt(jnp.mean(xfloat * xfloat, -1, keepdims=True) + eps)
    weighted = dnormed * gain_full
    dx = rstd * weighted - xfloat * rstd**3 * jnp.mean(weighted * xfloat, -1, keepdims=True)
    tokens_grad = (cot.astype(f32) + dx)[None]

    (outproj_grad,) = call(
        2,
        lambda *r: outer_kernel(dims, *r),
        [idx] + zo_all,
        [((contexts * channels, rows), f32)],
        [],
    )
    shared = sum(p[:, channels : channels + state].astype(f32) for p in fx)
    bc_half = shared.astype(bf16)
    bc_away = swap(bc_half, "tensor", 1)
    bcproj_grad = jnp.concatenate(
        [jnp.where(t == 0, bc_half, bc_away), jnp.where(t == 0, bc_away, bc_half)], 1
    ).astype(f32)
    piece = head // shards
    names = contexts * heads
    final = call(
        4,
        lambda *r: final_kernel(dims, *r),
        [idx] + zo_all + fx,
        [
            ((rows, 2, contexts * channels), f32),
            ((rows, names), f32),
            ((1, rows), f32),
            ((CONV, names, piece), f32),
            ((names, piece), f32),
            ((names, piece), f32),
            ((CONV, bcw // shards), f32),
            ((1, bcw // shards), f32),
            ((1, names), f32),
            ((1, names), f32),
            ((1, names), f32),
        ],
        [],
    )
    inproj_grad, dtproj_grad, ng, convw_grad, convb_grad, outgain_grad, bcconv_grad = final[:7]
    return (
        block_out,
        tokens_grad,
        ng.reshape(-1),
        inproj_grad,
        bcproj_grad,
        dtproj_grad,
        convw_grad,
        convb_grad,
        bcconv_grad,
        final[7].reshape(-1),
        final[8].reshape(-1),
        final[9].reshape(-1),
        final[10].reshape(-1),
        outgain_grad,
        outproj_grad,
    )


def solution(mesh):
    return jax.shard_map(
        layer,
        mesh=mesh,
        in_specs=(
            P("shard", "context", None),
            P("shard", None),
            P("shard"),
            P("shard", None, "tensor"),
            P("shard", None),
            P("shard", "tensor"),
            P(None, "tensor", "shard"),
            P("tensor", "shard"),
            P(None, "shard"),
            P("shard"),
            P("tensor"),
            P("tensor"),
            P("tensor"),
            P("tensor", "shard"),
            P("tensor", "shard"),
            P("shard", "context", None),
        ),
        out_specs=(
            P("shard", "context", "tensor"),
            P("shard", "context", None),
            P("shard"),
            P("shard", None, "tensor"),
            P("shard", None),
            P("shard", "tensor"),
            P(None, "tensor", "shard"),
            P("tensor", "shard"),
            P(None, "shard"),
            P("shard"),
            P("tensor"),
            P("tensor"),
            P("tensor"),
            P("tensor", "shard"),
            P("tensor", "shard"),
        ),
        check_vma=False,
    )
```

```python
import jax
import jax.numpy as jnp
from jax import lax
from jax.experimental import pallas as pl
from jax.experimental.pallas import tpu as pltpu
from jax.sharding import PartitionSpec as P

CONV = 4
SPAN = 128
PAD = 16
GAIN = 8
HEADP = 16
BCP = 24
RATE = 40
BCLO = 32
MISC = 128
eps = 1e-05
f32 = jnp.float32
bf16 = jnp.bfloat16


def mm(a, b, ca=1, cb=0):
    return lax.dot_general(a, b, (((ca,), (cb,)), ((), ())), preferred_element_type=f32)


def pieces(x, count):
    parts = []
    for _ in range(count):
        part = x.astype(bf16)
        parts.append(part)
        x = x - part.astype(f32)
    return parts


def mm3(a, b, ca=1, cb=0):
    ah, al = pieces(a, 2)
    bh, bl = pieces(b, 2)
    return mm(ah, bh, ca, cb) + (mm(al, bh, ca, cb) + mm(ah, bl, ca, cb))


def exact_left(ones, x, count, cb=0):
    return sum(mm(ones, part, 1, cb) for part in pieces(x, count))


def exact_right(x, ones, count, ca=1, cb=0):
    return sum(mm(part, ones, ca, cb) for part in pieces(x, count))


def iota(shape, dim):
    return lax.broadcasted_iota(jnp.int32, shape, dim)


def low(x, size):
    return lax.bitwise_and(x, jnp.int32(size - 1))


def high(x, size):
    return lax.shift_right_logical(x, jnp.int32(size.bit_length() - 1))


def sigmoid(x):
    return 1.0 / (1.0 + jnp.exp(-x))


def softplus(x):
    return jnp.maximum(x, 0.0) + jnp.log1p(jnp.exp(-jnp.abs(x)))


def spread_head(width, shards, channels, head):
    rows = width // shards
    part = head // shards
    used = (channels // head) * part
    r, c = iota((width, channels), 0), iota((width, channels), 1)
    s, q = high(r, rows), low(r, rows)
    hit = (c == high(q, part) * head + s * part + low(q, part)) & (q < used)
    return hit.astype(f32).astype(bf16)


def spread_bc(width, shards, channels):
    rows = width // shards
    part = channels // shards
    r, c = iota((width, channels), 0), iota((width, channels), 1)
    s, q = high(r, rows), low(r, rows)
    return ((c == s * part + q) & (q < part)).astype(f32).astype(bf16)


def spread_rate(width, shards, channels, head):
    rows = width // shards
    r, c = iota((width, channels), 0), iota((width, channels), 1)
    q = low(r, rows)
    return ((c == q * head) & (q < channels // head)).astype(f32).astype(bf16)


def block_ones(channels, head):
    r, c = iota((channels, channels), 0), iota((channels, channels), 1)
    return (high(r, head) == high(c, head)).astype(f32).astype(bf16)


def one_hot(rows, cols, row, col):
    return ((iota((rows, cols), 0) == row) & (iota((rows, cols), 1) == col)).astype(f32).astype(bf16)


def triangle(lower):
    r, c = iota((SPAN, SPAN), 0), iota((SPAN, SPAN), 1)
    hit = (r >= c) if lower else (r <= c)
    return hit.astype(f32).astype(bf16)


def local_decay(keep, a, at, head, h):
    diff = a[:, h * head : h * head + 1] - at[h * head : h * head + 1, :]
    return jnp.exp(jnp.where(keep, diff, -1e30))


def at_rows(start, size, by):
    return pl.ds(pl.multiple_of(start, by), size)


class Rows:
    def __init__(self, source, target, sems, size):
        self.source, self.target, self.sems, self.size = source, target, sems, size

    def copy(self, i):
        at = at_rows(i * self.size, self.size, self.size)
        return pltpu.make_async_copy(self.source.at[at], self.target.at[at], self.sems.at[i])

    def start(self, i):
        self.copy(i).start()

    def wait(self, i):
        self.copy(i).wait()


def front_kernel(dims, *refs):
    shards, contexts, head, channels, state = dims
    it = iter(refs)
    idx = next(it)
    segr, masks, rates = next(it), next(it), next(it)
    own = next(it)
    cown = next(it)
    mine = [next(it) for _ in range(contexts - 1)]
    other = [next(it) for _ in range(contexts - 1)]
    wparts = [next(it) for _ in range(shards)]
    mparts = [next(it) for _ in range(shards)]
    bcother = next(it)
    small, *houts, cot = (next(it) for _ in range(9))
    wdt, sref, pref, xtok, xcot = (next(it) for _ in range(5))
    normed, wfull, pre, uall, dtraw, ssd, states = (next(it) for _ in range(7))
    tsem, csem, nsem, psem, vsem, once = (next(it) for _ in range(6))
    put_cot = pltpu.make_async_copy(xcot, cot, once.at[2])
    hnormed, hwfull, hpre, huall, hdtraw, hssd, hstates = houts
    c, t, s = idx[0], idx[1], idx[2]
    length, width = own.shape
    half = length // 2
    total = length * contexts
    rows = width // shards
    bcw = 2 * state
    spans = [(at_rows(c * length, length, length), own, cown)]
    for k in range(1, contexts):
        base = (c ^ k) * length
        spans.append((at_rows(base + t * half, half, half), mine[k - 1], None))
        spans.append((at_rows(base + (1 - t) * half, half, half), other[k - 1], None))
    loads, moves = [], []
    for n, (where, token, cots) in enumerate(spans):
        head_rows = token if cots is not None else token.at[pl.ds(0, half)]
        tail_rows = cots if cots is not None else token.at[pl.ds(half, half)]
        loads.append(pltpu.make_async_copy(head_rows, xtok.at[where], tsem.at[n]))
        moves.append(pltpu.make_async_copy(tail_rows, xcot.at[where], csem.at[n]))
    for copy in loads + moves:
        copy.start()
    for k in range(shards):
        at = pl.multiple_of((s ^ k) * rows, rows)
        part = mparts[k]
        wfull[pl.ds(at, rows), 0:channels] = wparts[k][...]
        here, there = part[:, 0:state], bcother[k]
        wfull[pl.ds(at, rows), channels : channels + state] = jnp.where(t == 0, here, there)
        wfull[pl.ds(at, rows), channels + state : channels + bcw] = jnp.where(t == 0, there, here)
        wfull[pl.ds(at, rows), channels + bcw :] = part[:, state:]
    misc = wfull[:, channels + bcw :]
    small[0:MISC, :] = mm(misc, spread_head(width, shards, channels, head), 0, 0)
    small[MISC:, :] = mm(misc, spread_bc(width, shards, bcw), 0, 0)
    expand = (iota((MISC, channels), 0) == high(iota((MISC, channels), 1), head)).astype(f32)
    wdt[...] = mm(misc, expand.astype(bf16)).astype(bf16)
    gain = mm(one_hot(8, MISC, 0, GAIN), misc, 1, 1)[0:1, :]

    def norm(tokens):
        x = tokens.astype(f32)
        return (x * lax.rsqrt(jnp.mean(x * x, -1, keepdims=True) + eps) * gain).astype(bf16)

    keep_w = pltpu.make_async_copy(wfull, hwfull, once.at[0])
    keep_w.start()
    stores = []
    for n, (where, _, _) in enumerate(spans):
        loads[n].wait()
        normed[where, :] = norm(xtok[where, :])
        stores.append(pltpu.make_async_copy(normed.at[where], hnormed.at[where], nsem.at[n]))
        stores[-1].start()
    pref[0:PAD, :] = jnp.zeros((PAD, channels + bcw), f32)
    pre[0:PAD, :] = jnp.zeros((PAD, channels + bcw), bf16)
    chunk = 2 * SPAN
    chunks = total // chunk
    blocks = total // SPAN
    first_pre = pltpu.make_async_copy(
        pre.at[pl.ds(0, PAD)], hpre.at[pl.ds(0, PAD)], once.at[1]
    )
    first_pre.start()
    rest = pl.ds(PAD, total)
    for copy in moves:
        copy.wait()
    put_cot.start()
    put_pre = Rows(pre.at[rest], hpre.at[rest], psem.at[0], chunk)
    put_dt = Rows(dtraw, hdtraw, psem.at[1], chunk)
    put_u = Rows(uall, huall, vsem.at[0], SPAN)
    put_ssd = Rows(ssd, hssd, vsem.at[1], SPAN)
    put_states = Rows(states, hstates, vsem.at[2], channels)

    def project(i, _):
        at = pl.multiple_of(i * chunk, chunk)
        n = normed[pl.ds(at, chunk), :]
        value = mm(n, wfull[:, 0 : channels + bcw]).astype(bf16)
        pre[pl.ds(pl.multiple_of(at + PAD, PAD), chunk), :] = value
        pref[pl.ds(pl.multiple_of(at + PAD, PAD), chunk), :] = value.astype(f32)
        dtraw[pl.ds(at, chunk), :] = mm(n, wdt[...])
        put_pre.start(i)
        put_dt.start(i)
        return 0

    lax.fori_loop(0, chunks, project, 0)
    sref[...] = jnp.zeros_like(sref)
    tri = triangle(True)
    causal = iota((SPAN, SPAN), 0) >= iota((SPAN, SPAN), 1)
    side = iota((SPAN, 2 * head), 1) < head

    def scan(i, _):
        at = pl.multiple_of(i * SPAN, SPAN)
        window = pref[pl.ds(at, SPAN + PAD), :]
        mk = masks[pl.ds(at, SPAN), :]
        taps = jnp.concatenate(
            [small[HEADP : HEADP + 8, :], small[MISC + BCP : MISC + BCP + 8, :]], 1
        )
        u = taps[CONV - 1 : CONV, :] * window[PAD:, :]
        bias = jnp.concatenate(
            [small[HEADP + 4 : HEADP + 5, :], small[MISC + BCP + 4 : MISC + BCP + 5, :]], 1
        )
        u = u + bias
        for j in range(1, CONV):
            u = u + taps[CONV - 1 - j : CONV - j, :] * (
                window[PAD - j : PAD - j + SPAN, :] * mk[:, j - 1 : j]
            )
        uall[pl.ds(at, SPAN), :] = u
        act = u * sigmoid(u)
        x = act[:, 0:channels]
        bfull, cfull = act[:, channels : channels + state], act[:, channels + state :]
        bb, cb = bfull.astype(bf16), cfull.astype(bf16)
        dt = softplus(dtraw[pl.ds(at, SPAN), :] + rates[0:1, :])
        a = exact_left(tri, rates[1:2, :] * dt, 3)
        att = a.T
        step = x * dt
        ub = step.astype(bf16)
        g = mm3(cfull, bfull, 1, 1)
        keep = (mk[:, 5:6] == segr[pl.ds(i, 1), :]) & causal
        inner = []
        for pair in range(channels // (2 * head)):
            up = ub[:, pair * 2 * head : (pair + 1) * 2 * head]
            both = [
                mm((g * local_decay(keep, a, att, head, 2 * pair + e)).astype(bf16), up)
                for e in range(2)
            ]
            inner.append(jnp.where(side, both[0], both[1]))
        before = sref[...]
        sb = before.astype(bf16)
        states[pl.ds(pl.multiple_of(i * channels, channels), channels), :] = sb
        carry = jnp.exp(a) * mk[:, 3:4]
        y = jnp.concatenate(inner, 1) + carry * mm(cb, sb, 1, 1)
        ssd[pl.ds(at, SPAN), :] = y + rates[2:3, :] * x
        tail = jnp.exp(a[SPAN - 1 :, :] - a) * mk[:, 4:5]
        through = jnp.exp(att[:, SPAN - 1 :]) * mk[SPAN - 1 :, 3:4]
        sref[...] = through * before + mm((tail * step).astype(bf16), bb, 0, 0)
        put_u.start(i)
        put_ssd.start(i)
        put_states.start(i)
        return 0

    lax.fori_loop(0, blocks, scan, 0)
    for copy in stores + [keep_w, first_pre, put_cot]:
        copy.wait()

    def finish_chunk(i, _):
        put_pre.wait(i)
        put_dt.wait(i)
        return 0

    def finish_block(i, _):
        put_u.wait(i)
        put_ssd.wait(i)
        put_states.wait(i)
        return 0

    lax.fori_loop(0, chunks, finish_chunk, 0)
    lax.fori_loop(0, blocks, finish_block, 0)


def gate_kernel(dims, *refs):
    shards, _, _, channels, _ = dims
    it = iter(refs)
    idx = next(it)
    normed, ssd, small, cot = next(it), next(it), next(it), next(it)
    wparts = [next(it) for _ in range(shards)]
    sums, wzo, zval, dyn = (next(it) for _ in range(4))
    s = idx[2]
    width = normed.shape[1]
    rows = width // shards
    for k in range(shards):
        wzo[pl.ds(pl.multiple_of((s ^ k) * rows, rows), rows), :] = wparts[k][...]
    chunk = 2 * SPAN
    ogain = small[HEADP + 5 : HEADP + 6, :]
    ones = jnp.ones((8, channels), bf16)
    for i in range(normed.shape[0] // chunk):
        at = slice(i * chunk, (i + 1) * chunk)
        z = mm(normed[at, :], wzo[:, 0:channels])
        d = mm(cot[at, :], wzo[:, channels:])
        zval[at, :] = z
        dyn[at, :] = d
        gated = ssd[at, :] * (z * sigmoid(z))
        sums[0:1, at] = exact_left(ones, gated * gated, 2, 1)[0:1, :]
        sums[1:2, at] = exact_left(ones, d * ogain * gated, 2, 1)[0:1, :]


def mid_kernel(dims, inner, *refs):
    shards, _, _, channels, _ = dims
    it = iter(refs)
    idx = next(it)
    sums, normed, ssd, small, cot, wzo, zval, dyn = (next(it) for _ in range(8))
    okeep, osend, dz, dssd, ogg, ngz = (next(it) for _ in range(6))
    gparts = [next(it) for _ in range(shards)]
    yref, gref = next(it), next(it)
    t, s = idx[1], idx[2]
    total, width = normed.shape
    rows = width // shards
    part = width // 2
    chunk = 2 * SPAN
    ogain = small[HEADP + 5 : HEADP + 6, :]
    first = (iota((8, channels), 0) == 0).astype(f32).astype(bf16)
    second = (iota((8, channels), 0) == 1).astype(f32).astype(bf16)
    gacc = jnp.zeros((1, channels), f32)
    keep_at = pl.multiple_of(t * part, part)
    send_at = pl.multiple_of((1 - t) * part, part)
    for i in range(total // chunk):
        at = slice(i * chunk, (i + 1) * chunk)
        pair = jnp.concatenate([sums[:, at], jnp.zeros((6, chunk), f32)], 0)
        square = exact_right(pair, first, 3, 0, 0)
        cross = exact_right(pair, second, 3, 0, 0)
        z = zval[at, :]
        sg = sigmoid(z)
        zs = z * sg
        out = ssd[at, :]
        gated = out * zs
        r = lax.rsqrt(square / inner + eps)
        ynorm = (gated * r * ogain).astype(bf16)
        yref[at, :] = ynorm
        okeep[at, :] = mm(ynorm, wzo[pl.ds(keep_at, part), channels:], 1, 1).astype(bf16)
        osend[at, :] = mm(ynorm, wzo[pl.ds(send_at, part), channels:], 1, 1).astype(bf16)
        d = dyn[at, :]
        dgated = r * (d * ogain) - gated * (r * r * r) * (cross / inner)
        dssd[at, :] = dgated * zs
        dz[at, :] = (dgated * out * (sg * (1.0 + z * (1.0 - sg)))).astype(bf16)
        gacc = gacc + jnp.sum(d * gated * r, 0, keepdims=True)
    ogg[...] = jnp.broadcast_to(gacc, ogg.shape)
    for i in range(width // chunk):
        at = slice(i * chunk, (i + 1) * chunk)
        gz = mm(normed[:, at], dz[...], 0, 0)
        dots = jnp.sum(gz * wzo[at, 0:channels].astype(f32), -1, keepdims=True)
        ngz[at, :] = jnp.broadcast_to(dots, (chunk, MISC))
        gref[at, 0:channels] = gz.astype(bf16)
        gref[at, channels:] = mm(cot[:, at], yref[...], 0, 0).astype(bf16)
    for k in range(shards):
        gparts[k][...] = gref[pl.ds(pl.multiple_of((s ^ k) * rows, rows), rows), :]


def scan_kernel(dims, *refs):
    _, _, head, channels, state = dims
    it = iter(refs)
    idx = next(it)
    segr, masks, rates = next(it), next(it), next(it)
    small, pre, huall, hdtraw, hssd, states, hdssd = (next(it) for _ in range(7))
    hdcat, acc, dsref = (next(it) for _ in range(3))
    uall, dtraw, ssd, dssd, dcat, sems, osem = (next(it) for _ in range(7))
    total = huall.shape[0]
    count = total // SPAN
    takes = [
        Rows(src, dst, sems.at[n], SPAN)
        for n, (src, dst) in enumerate(
            ((huall, uall), (hdtraw, dtraw), (hdssd, dssd), (hssd, ssd))
        )
    ]
    give = Rows(dcat, hdcat, osem, SPAN)
    for i in reversed(range(count)):
        for take in takes:
            take.start(i)
    bcw = 2 * state
    cat = channels + bcw
    blocks = total // SPAN
    dsref[...] = jnp.zeros_like(dsref)
    acc[...] = jnp.zeros_like(acc)
    lower, upper = triangle(True), triangle(False)
    ones = block_ones(channels, head)
    causal = iota((SPAN, SPAN), 0) >= iota((SPAN, SPAN), 1)
    side = iota((SPAN, 2 * head), 1) < head
    last = iota((SPAN, channels), 0) == SPAN - 1
    sel = (
        iota((channels, MISC), 0) == iota((channels, MISC), 1) * head
    ).astype(f32).astype(bf16)
    row8 = jnp.ones((8, state), bf16)

    def step(ii, halo):
        i = blocks - 1 - ii
        at = pl.multiple_of(i * SPAN, SPAN)
        here = pl.ds(at, SPAN)
        for take in takes:
            take.wait(i)
        mk = masks[pl.ds(at, SPAN + PAD), :]
        mh = mk[0:SPAN, :]
        u = uall[here, :]
        sg = sigmoid(u)
        act = u * sg
        x = act[:, 0:channels]
        bfull, cfull = act[:, channels : channels + state], act[:, channels + state :]
        bb, cb = bfull.astype(bf16), cfull.astype(bf16)
        raw = dtraw[here, :] + rates[0:1, :]
        dt = softplus(raw)
        dec = rates[1:2, :] * dt
        a = exact_left(lower, dec, 3)
        att = a.T
        us = x * dt
        ub = us.astype(bf16)
        dy = dssd[here, :]
        dyb = dy.astype(bf16)
        g = mm3(cfull, bfull, 1, 1)
        keep = (mh[:, 5:6] == segr[pl.ds(i, 1), :]) & causal
        carry = jnp.exp(a) * mh[:, 3:4]
        tail = jnp.exp(a[SPAN - 1 :, :] - a) * mh[:, 4:5]
        sb = states[pl.ds(pl.multiple_of(i * channels, channels), channels), :]
        nxt = jnp.minimum(i + 1, blocks - 1)
        snext = states[pl.ds(pl.multiple_of(nxt * channels, channels), channels), :].astype(f32)
        dsn = dsref[...]
        dsb = dsn.astype(bf16)
        cdy = carry * dy
        tu = tail * us
        dg = jnp.zeros((SPAN, SPAN), f32)
        dus = []
        for pair in range(channels // (2 * head)):
            lanes = slice(pair * 2 * head, (pair + 1) * 2 * head)
            dyp = dyb[:, lanes]
            both = []
            for e in range(2):
                decay = local_decay(keep, a, att, head, 2 * pair + e)
                mine = side if e == 0 else jnp.logical_not(side)
                dm = mm3(dy[:, lanes], jnp.where(mine, us[:, lanes], 0.0), 1, 1)
                dg = dg + dm * decay
                both.append(mm((g * decay).astype(bf16), dyp, 0, 0))
            dus.append(jnp.where(side, both[0], both[1]))
        dc = mm3(dg, bfull) + exact_right(cdy, sb, 2)
        db = mm3(dg, cfull, 0, 0) + mm3(tu, dsn)
        du = jnp.concatenate(dus, 1) + tail * mm(bb, dsb, 1, 1)
        through = jnp.exp(att[:, SPAN - 1 :]) * mh[SPAN - 1 :, 3:4]
        dsref[...] = through * dsn + mm(cdy.astype(bf16), cb, 0, 0)
        y = ssd[here, :] - rates[2:3, :] * x
        extra = exact_left(row8, snext * dsn, 3, 1)[0:1, :]
        e = dyb.astype(f32) * y - ub.astype(f32) * du
        e = e + jnp.where(last, extra, 0.0)
        ddec = exact_right(exact_left(upper, e, 3), ones, 3)
        xdu = exact_right(x * du, ones, 2)
        ddt = (xdu + rates[1:2, :] * ddec) * sigmoid(raw)
        acc[8:9, :] = acc[8:9, :] + jnp.sum(ddt, 0, keepdims=True)
        acc[9:10, :] = acc[9:10, :] + jnp.sum(ddec * dec, 0, keepdims=True)
        acc[10:11, :] = acc[10:11, :] + jnp.sum(dy * x, 0, keepdims=True)
        dx = dt * du + rates[2:3, :] * dy
        dact = jnp.concatenate([dx, db, dc], 1)
        dut = dact * (sg * (1.0 + u * (1.0 - sg)))
        dwin = jnp.concatenate([dut, halo], 0)
        pwin = pre[pl.ds(at, SPAN + PAD), :].astype(f32)
        taps = jnp.concatenate(
            [small[HEADP : HEADP + 8, :], small[MISC + BCP : MISC + BCP + 8, :]], 1
        )
        dpre = taps[CONV - 1 : CONV, :] * dut

        def gather(row, value):
            total_row = jnp.sum(value, 0, keepdims=True)
            acc[row : row + 1, :] = acc[row : row + 1, :] + total_row[:, 0:channels]
            acc[16 + row : 17 + row, 0:bcw] = acc[16 + row : 17 + row, 0:bcw] + total_row[:, channels:]

        gather(CONV - 1, dut * pwin[PAD:, :])
        gather(CONV, dut)
        for j in range(1, CONV):
            moved = dwin * mk[:, j - 1 : j]
            dpre = dpre + taps[CONV - 1 - j : CONV - j, :] * moved[j : j + SPAN, :]
            gather(CONV - 1 - j, moved[0:SPAN, :] * pwin[PAD - j : PAD - j + SPAN, :])
        dcat[here, 0:cat] = dpre.astype(bf16)
        dcat[here, cat:] = mm(ddt.astype(bf16), sel).astype(bf16)
        give.start(i)
        return dut[0:PAD, :]

    lax.fori_loop(0, blocks, step, jnp.zeros((PAD, cat), f32))
    acc[8:16, :] = jnp.where(
        iota((8, channels), 0) == 2, exact_right(acc[8:16, :], ones, 3), acc[8:16, :]
    )

    def finish(i, _):
        give.wait(i)
        return 0

    lax.fori_loop(0, blocks, finish, 0)


def token_kernel(dims, *refs):
    _, _, _, channels, _ = dims
    idx, wfull, wzo, dz, dcat, dkeep, dsend = refs
    t = idx[1]
    total, width = dcat.shape[0], wfull.shape[0]
    part = width // 2
    chunk = 2 * SPAN
    for i in range(total // chunk):
        at = slice(i * chunk, (i + 1) * chunk)
        full = mm(dcat[at, :], wfull[...], 1, 1) + mm(dz[at, :], wzo[:, 0:channels], 1, 1)
        lo, hi = full[:, 0:part].astype(bf16), full[:, part:].astype(bf16)
        dkeep[at, :] = jnp.where(t == 0, lo, hi)
        dsend[at, :] = jnp.where(t == 0, hi, lo)


def weight_kernel(dims, *refs):
    shards, _, head, channels, state = dims
    idx, normed, wfull, dcat, acc, ogg, ngz, gkeep, gsend = refs[:9]
    gparts, gref = refs[9:-1], refs[-1]
    t, s = idx[1], idx[2]
    width = wfull.shape[0]
    rows = width // shards
    bcw = 2 * state
    cat = channels + bcw
    chunk = 2 * SPAN
    headg = jnp.where(iota((8, channels), 0) == 5, ogg[0:8, :], acc[0:8, :])
    z8 = jnp.zeros((8, channels), f32)

    def place(rowsets, spread):
        stack = [z8] * (MISC // 8)
        for row, value in rowsets:
            stack[row // 8] = value
        return mm(spread, jnp.concatenate(stack, 0).astype(bf16), 1, 1)

    misc = place([(HEADP, headg)], spread_head(width, shards, channels, head))
    bch, bcl = pieces(acc[16:24, 0:bcw], 2)
    misc = misc + place(
        [(BCP, bch.astype(f32)), (BCLO, bcl.astype(f32))], spread_bc(width, shards, bcw)
    )
    misc = misc + place([(RATE, acc[8:16, :])], spread_rate(width, shards, channels, head))
    gain_lane = (iota((1, MISC), 1) == GAIN).astype(f32)
    for i in range(width // chunk):
        at = slice(i * chunk, (i + 1) * chunk)
        gw = mm(normed[:, at], dcat[...], 0, 0)
        w = wfull[at, :].astype(f32)
        ng = jnp.sum(gw * w, -1, keepdims=True) + ngz[at, 0:1]
        ng = ng / w[:, cat + GAIN : cat + GAIN + 1]
        gref[at, :] = gw[:, 0:channels].astype(bf16)
        b, c = gw[:, channels : channels + state], gw[:, channels + state : cat]
        gkeep[at, 0:state] = jnp.where(t == 0, b, c).astype(bf16)
        gsend[at, 0:state] = jnp.where(t == 0, c, b).astype(bf16)
        m = (gw[:, cat:] + misc[at, :] + ng * gain_lane).astype(bf16)
        gkeep[at, state:] = m
        gsend[at, state:] = m
    for k in range(shards):
        gparts[k][...] = gref[pl.ds(pl.multiple_of((s ^ k) * rows, rows), rows), :]


def outer_kernel(dims, *refs):
    _, contexts, _, channels, _ = dims
    idx, parts, out = refs[0], refs[1:-1], refs[-1]
    for k in range(contexts):
        at = pl.multiple_of((idx[0] ^ k) * channels, channels)
        out[pl.ds(at, channels), :] = parts[k][:, channels:].astype(f32).T


def final_kernel(dims, *refs):
    shards, contexts, head, channels, state = dims
    idx = refs[0]
    zparts, xparts = refs[1 : 1 + contexts], refs[1 + contexts : 1 + 2 * contexts]
    gi, dt, ng, cw, cb, og, bcc, bcb, ra, rb, rc = refs[1 + 2 * contexts :]
    c = idx[0]
    rows = gi.shape[0]
    heads = channels // head
    piece = head // shards
    span = heads * piece
    every = contexts * span
    names = contexts * heads
    pick = iota((8, MISC), 1)
    line = iota((8, MISC), 0)
    bcsel = ((pick == line + BCP) | (pick == line + BCLO)) & (line < 5)
    bcsel = bcsel.astype(f32).astype(bf16)
    gsel = one_hot(8, MISC, 0, GAIN)
    dts = jnp.zeros((names, rows), f32)
    gains = jnp.zeros((8, rows), f32)
    bcs = jnp.zeros((8, rows), f32)
    small = jnp.zeros((MISC, every), f32)
    rates = jnp.zeros((MISC, names), f32)
    for k in range(contexts):
        place = c ^ k
        at = pl.multiple_of(place * channels, channels)
        gi[:, 0, pl.ds(at, channels)] = zparts[k][:, 0:channels].astype(f32)
        gi[:, 1, pl.ds(at, channels)] = xparts[k][:, 0:channels].astype(f32)
        m = xparts[k][:, channels + state :]

        def to_lane(count, width, size):
            r, q = iota((count, width), 0), iota((count, width), 1)
            return ((q == place * size + r) & (r < size)).astype(f32).astype(bf16)

        r, q = iota((names, MISC), 0), iota((names, MISC), 1)
        lift = ((r == place * heads + q) & (q < heads)).astype(f32).astype(bf16)
        dts = dts + mm(lift, m, 1, 1)
        gains = gains + mm(gsel, m, 1, 1)
        bcs = bcs + mm(bcsel, m, 1, 1)
        small = small + mm(m, to_lane(rows, every, span), 0, 0)
        rates = rates + mm(m, to_lane(rows, names, heads), 0, 0)
    dt[...] = dts
    ng[...] = gains[0:1, :]
    bcc[...] = bcs[0:CONV, 0 : bcc.shape[1]]
    bcb[...] = bcs[CONV : CONV + 1, 0 : bcb.shape[1]]
    mine = high(iota((names, every), 1), piece) == iota((names, every), 0)
    fold = (low(iota((every, piece), 0), piece) == iota((every, piece), 1)).astype(f32).astype(bf16)

    def split(row):
        return mm(jnp.where(mine, small[row : row + 1, :], 0.0).astype(bf16), fold)

    for j in range(CONV):
        cw[j] = split(HEADP + j)
    cb[...] = split(HEADP + CONV)
    og[...] = split(HEADP + CONV + 1)
    for j, ref in enumerate((ra, rb, rc)):
        ref[...] = rates[RATE + j : RATE + j + 1, :]


def swap(x, axis, k):
    return lax.ppermute(x, axis, [(i, i ^ k) for i in range(lax.axis_size(axis))])


def call(cost, body, args, outs, scratch, far_in=(), far_out=()):
    smem = pl.BlockSpec(memory_space=pltpu.SMEM)
    vmem = pl.BlockSpec(memory_space=pltpu.VMEM)
    far = pl.BlockSpec(memory_space=pl.ANY)
    ins = [smem] + [far if i in far_in else vmem for i in range(1, len(args))]
    out = [far if i in far_out else vmem for i in range(len(outs))]
    return launch(cost, body, args, outs, scratch, ins, out)


def launch(cost, body, args, outs, scratch, ins, out):
    return pl.pallas_call(
        body,
        cost_estimate=pl.CostEstimate(flops=cost * 10**9, transcendentals=0, bytes_accessed=1 << 20),
        out_shape=[jax.ShapeDtypeStruct(s, d) for s, d in outs],
        in_specs=ins,
        out_specs=out,
        scratch_shapes=[
            pltpu.SemaphoreType.DMA(s) if d is None else pltpu.VMEM(s, d) for s, d in scratch
        ],
        compiler_params=pltpu.CompilerParams(vmem_limit_bytes=56 << 20),
    )(*args)


def layer(
    tokens,
    segment_ids,
    norm_gain,
    in_proj,
    bc_proj,
    dt_proj,
    conv_weight,
    conv_bias,
    bc_conv,
    bc_bias,
    dt_bias,
    a_log,
    d_skip,
    out_gain,
    out_proj,
    cotangent,
):
    shards, contexts = lax.axis_size("shard"), lax.axis_size("context")
    s, c, t = lax.axis_index("shard"), lax.axis_index("context"), lax.axis_index("tensor")
    idx = jnp.stack([c, t, s]).astype(jnp.int32)
    length, width = tokens.shape[1:]
    total = length * contexts
    rows = in_proj.shape[0]
    heads = dt_bias.shape[0] // contexts
    state = bc_proj.shape[1] // 2
    bcw = 2 * state
    channels = in_proj.shape[2] // contexts
    head = channels // heads
    inner = in_proj.shape[2] * lax.axis_size("tensor")
    dims = (shards, contexts, head, channels, state)
    own, cot = tokens[0], cotangent[0]

    def mine(x, dim, size):
        return lax.dynamic_slice_in_dim(x, c * size, size, dim)

    half = length // 2
    pair = jnp.concatenate(
        [lax.dynamic_slice_in_dim(x, t * half, half, 0) for x in (own, cot)], 0
    )
    tok_mine = [swap(pair, "context", k) for k in range(1, contexts)]
    both = lax.dynamic_slice(in_proj, (0, 0, c * channels), (rows, 2, channels))
    hparts = [
        mine(conv_weight, 1, heads).reshape(CONV, -1),
        mine(conv_bias, 0, heads).reshape(1, -1),
        mine(out_gain, 0, heads).reshape(1, -1),
    ]
    headp = jnp.concatenate(hparts, 0).T
    bcp = jnp.concatenate([bc_conv, bc_bias[None]], 0).T

    def column(x, at):
        return jnp.pad(x, ((0, rows - x.shape[0]), (at, MISC - at - x.shape[1])))

    misc = (
        column(mine(dt_proj, 1, heads), 0)
        + column(norm_gain[:, None], GAIN)
        + column(headp, HEADP)
        + column(bcp, BCP)
    )
    wx = both[:, 1]
    wx_parts = [wx] + [swap(wx, "shard", k) for k in range(1, shards)]
    wm = jnp.concatenate([lax.dynamic_slice_in_dim(bc_proj, t * state, state, 1), misc], 1)
    wm_parts = [wm] + [swap(wm, "shard", k) for k in range(1, shards)]
    bc_other = swap(jnp.stack([w[:, :state] for w in wm_parts]), "tensor", 1)
    tok_other = [swap(x, "tensor", 1) for x in tok_mine]
    wo = mine(out_proj, 0, channels).T
    wb = jnp.concatenate([both[:, 0], wo], 1)
    wb_parts = [wb] + [swap(wb, "shard", k) for k in range(1, shards)]

    seg = segment_ids[0]
    cols = []
    for j in range(1, CONV):
        moved = jnp.concatenate([jnp.full((j,), -1, jnp.int32), seg[:-j]])
        cols.append((moved == seg).astype(f32))
    grid = seg.reshape(total // SPAN, SPAN)
    previous = jnp.concatenate([jnp.full((1,), -1, jnp.int32), grid[:-1, -1]])
    cols.append((grid == previous[:, None]).astype(f32).reshape(-1))
    cols.append((grid == grid[:, -1:]).astype(f32).reshape(-1))
    cols.append(seg.astype(f32))
    masks = jnp.pad(jnp.stack(cols, 1), ((0, PAD), (0, 2)))
    segr = grid.astype(f32)
    rates = jnp.stack([mine(dt_bias, 0, heads), -jnp.exp(mine(a_log, 0, heads)), mine(d_skip, 0, heads)])
    rates = jnp.pad(jnp.repeat(rates, head, axis=1), ((0, 5), (0, 0)))

    cat = channels + bcw
    kept = [
        ((total, width), bf16),
        ((width, cat + MISC), bf16),
        ((total + PAD, cat), bf16),
        ((total, cat), f32),
        ((total, channels), f32),
        ((total, channels), f32),
        ((total // SPAN * channels, state), bf16),
    ]
    front = call(
        15,
        lambda *r: front_kernel(dims, *r),
        [idx, segr, masks, rates, own, cot]
        + tok_mine
        + tok_other
        + wx_parts
        + wm_parts
        + [bc_other],
        [((2 * MISC, channels), f32)] + kept + [((total, width), bf16)],
        [
            ((width, channels), bf16),
            ((channels, state), f32),
            ((total + PAD, cat), f32),
            ((total, width), bf16),
            ((total, width), bf16),
        ]
        + kept
        + [
            ((2 * contexts - 1,), None),
            ((2 * contexts - 1,), None),
            ((2 * contexts - 1,), None),
            ((2, total // (2 * SPAN)), None),
            ((3, total // SPAN), None),
            ((3,), None),
        ],
        far_in=range(4, 4 + 2 * contexts),
        far_out=range(1, 9),
    )
    small, normed, wfull, pre, uall, dtraw, ssd, states, cotfull = front
    sums, wzo, zval, dyn = call(
        7,
        lambda *r: gate_kernel(dims, *r),
        [idx, normed, ssd, small, cotfull] + wb_parts,
        [
            ((2, total), f32),
            ((width, 2 * channels), bf16),
            ((total, channels), f32),
            ((total, channels), f32),
        ],
        [],
    )
    sums = sums + swap(sums, "tensor", 1)
    k = 1
    while k < contexts:
        sums = sums + swap(sums, "context", k)
        k *= 2
    part = width // 2
    mid = call(
        8,
        lambda *r: mid_kernel(dims, inner, *r),
        [idx, sums, normed, ssd, small, cotfull, wzo, zval, dyn],
        [
            ((total, part), bf16),
            ((total, part), bf16),
            ((total, channels), bf16),
            ((total, channels), f32),
            ((8, channels), f32),
            ((width, MISC), f32),
        ]
        + [((rows, 2 * channels), bf16)] * shards,
        [((total, channels), bf16), ((width, 2 * channels), bf16)],
    )
    okeep, osend, dz, dssd, ogg, ngz = mid[:6]
    zo = mid[6:]

    def stream_reduce(keep, send):
        away = swap(send, "tensor", 1)
        full = keep.astype(f32) + away.astype(f32)

        def rows_of(k):
            return lax.dynamic_slice_in_dim(full, (c ^ k) * length, length, 0)

        got = [swap(rows_of(k).astype(bf16), "context", k) for k in range(1, contexts)]
        return rows_of(0) + sum(g.astype(f32) for g in got)

    def shard_reduce(parts):
        got = [swap(parts[k], "shard", k) for k in range(1, shards)]
        return (parts[0].astype(f32) + sum(g.astype(f32) for g in got)).astype(bf16)

    def context_gather(x):
        return [x] + [swap(x, "context", k) for k in range(1, contexts)]

    mixed = stream_reduce(okeep, osend)
    residual = lax.dynamic_slice_in_dim(own, t * part, part, 1).astype(f32)
    block_out = (residual + mixed).astype(bf16)[None]
    zo_all = context_gather(shard_reduce(zo))

    dcat, acc = call(
        22,
        lambda *r: scan_kernel(dims, *r),
        [idx, segr, masks, rates, small, pre, uall, dtraw, ssd, states, dssd],
        [((total, cat + MISC), bf16), ((24, channels), f32)],
        [
            ((channels, state), f32),
            ((total, cat), f32),
            ((total, channels), f32),
            ((total, channels), f32),
            ((total, channels), f32),
            ((total, cat + MISC), bf16),
            ((4, total // SPAN), None),
            ((total // SPAN,), None),
        ],
        far_in=(6, 7, 8, 10),
        far_out=(0,),
    )
    gkeep, gsend, *gx = call(
        4,
        lambda *r: weight_kernel(dims, *r),
        [idx, normed, wfull, dcat, acc, ogg, ngz],
        [((width, state + MISC), bf16)] * 2 + [((rows, channels), bf16)] * shards,
        [((width, channels), bf16)],
    )
    dkeep, dsend = call(
        4,
        lambda *r: token_kernel(dims, *r),
        [idx, wfull, wzo, dz, dcat],
        [((total, part), bf16), ((total, part), bf16)],
        [],
    )
    lane = jnp.arange(MISC)
    common = (lane == GAIN) | ((lane >= BCP) & (lane < BCLO + 8))
    grecv = swap(gsend, "tensor", 1).astype(f32)
    grecv = jnp.concatenate([grecv[:, :state], jnp.where(common, grecv[:, state:], 0.0)], 1)
    gfull = gkeep.astype(f32) + grecv
    gparts = [
        lax.dynamic_slice_in_dim(gfull, (s ^ k) * rows, rows, 0).astype(bf16) for k in range(shards)
    ]
    gx = shard_reduce(gx)
    gm = shard_reduce(gparts)
    fx = context_gather(jnp.concatenate([gx, gm], 1))
    dpart = stream_reduce(dkeep, dsend)
    dpart = dpart.astype(bf16)
    dother = swap(dpart, "tensor", 1)
    dnormed = jnp.concatenate(
        [jnp.where(t == 0, dpart, dother), jnp.where(t == 0, dother, dpart)], 1
    ).astype(f32)

    xfloat = own.astype(f32)
    gain_full = wfull[:, cat + GAIN].astype(f32)
    rstd = lax.rsqrt(jnp.mean(xfloat * xfloat, -1, keepdims=True) + eps)
    weighted = dnormed * gain_full
    dx = rstd * weighted - xfloat * rstd**3 * jnp.mean(weighted * xfloat, -1, keepdims=True)
    tokens_grad = (cot.astype(f32) + dx)[None]

    (outproj_grad,) = call(
        2,
        lambda *r: outer_kernel(dims, *r),
        [idx] + zo_all,
        [((contexts * channels, rows), f32)],
        [],
    )
    shared = sum(p[:, channels : channels + state].astype(f32) for p in fx)
    bc_half = shared.astype(bf16)
    bc_away = swap(bc_half, "tensor", 1)
    bcproj_grad = jnp.concatenate(
        [jnp.where(t == 0, bc_half, bc_away), jnp.where(t == 0, bc_away, bc_half)], 1
    ).astype(f32)
    piece = head // shards
    names = contexts * heads
    final = call(
        4,
        lambda *r: final_kernel(dims, *r),
        [idx] + zo_all + fx,
        [
            ((rows, 2, contexts * channels), f32),
            ((names, rows), f32),
            ((1, rows), f32),
            ((CONV, names, piece), f32),
            ((names, piece), f32),
            ((names, piece), f32),
            ((CONV, bcw // shards), f32),
            ((1, bcw // shards), f32),
            ((1, names), f32),
            ((1, names), f32),
            ((1, names), f32),
        ],
        [],
    )
    inproj_grad, dtproj_grad, ng, convw_grad, convb_grad, outgain_grad, bcconv_grad = final[:7]
    return (
        block_out,
        tokens_grad,
        ng.reshape(-1),
        inproj_grad,
        bcproj_grad,
        dtproj_grad.T,
        convw_grad,
        convb_grad,
        bcconv_grad,
        final[7].reshape(-1),
        final[8].reshape(-1),
        final[9].reshape(-1),
        final[10].reshape(-1),
        outgain_grad,
        outproj_grad,
    )


def solution(mesh):
    return jax.shard_map(
        layer,
        mesh=mesh,
        in_specs=(
            P("shard", "context", None),
            P("shard", None),
            P("shard"),
            P("shard", None, "tensor"),
            P("shard", None),
            P("shard", "tensor"),
            P(None, "tensor", "shard"),
            P("tensor", "shard"),
            P(None, "shard"),
            P("shard"),
            P("tensor"),
            P("tensor"),
            P("tensor"),
            P("tensor", "shard"),
            P("tensor", "shard"),
            P("shard", "context", None),
        ),
        out_specs=(
            P("shard", "context", "tensor"),
            P("shard", "context", None),
            P("shard"),
            P("shard", None, "tensor"),
            P("shard", None),
            P("shard", "tensor"),
            P(None, "tensor", "shard"),
            P("tensor", "shard"),
            P(None, "shard"),
            P("shard"),
            P("tensor"),
            P("tensor"),
            P("tensor"),
            P("tensor", "shard"),
            P("tensor", "shard"),
        ),
        check_vma=False,
    )
```
